512 devices in a mesh: dp: 8 (over x, z_hi), wide: 64 (over y, z_lo, core).
Axes of the slice: x: 4, y: 4, z: 16 (z_hi: 2, z_lo: 8; z = z_hi * 8 + z_lo), core: 2. Of those that a mesh axis runs over, the one named last changes fastest.
Arguments:
- latents: bfloat16 [8, 128, 8, 16, 256], P('dp', 'wide'), may hold values from -36 to 36
- cotangent: bfloat16 [8, 128, 8, 16, 256], P('dp', 'wide'), may hold values from -41 to 41
- norm_gain: float32 [256], replicated, may hold values from 0.25 to 1.75
- norm_bias: float32 [256], replicated, may hold values from -3 to 3
- w_spatial: bfloat16 [2304, 256], P('dp'), may hold values from -0.125 to 0.125
- w_temporal: bfloat16 [768, 256], P('dp'), may hold values from -0.21875 to 0.21875
Outputs:
- block_out: bfloat16 [8, 128, 8, 16, 256], P('dp', 'wide')
- grad_latents: bfloat16 [8, 128, 8, 16, 256], P('dp', 'wide')
- grad_spatial: float32 [2304, 256], P('dp', 'wide')
- grad_temporal: float32 [768, 256], P('dp', 'wide')
- grad_norm: float32 [2, 256], P(None, 'wide')
The draws below stay inside these ranges and needn't reach their ends.
All inputs are finite; a program needn't handle non-finite values.
Results may differ from the reference program's by a relative error of at most 0.012.
Values may be sent and summed in bfloat16 or wider, within the bound.
A program may use at most 64 MiB of HBM per device.

```python
import math
import jax
import jax.numpy as jnp
from jax import lax

C = 256
GROUPS = 32
F_DEV = 2
ROWS = 8
COLS = 16
CLIPS = 8
FRAMES = 128


def draw_latents(key, part):
    key_noise, key_frame, key_chan = jax.random.split(key, 3)
    shape = (CLIPS, FRAMES, ROWS, COLS, C)
    position = jnp.arange(FRAMES).astype(jnp.float32) / (FRAMES - 1)
    ramp = jnp.exp(math.log(3.0) * position)
    jitter = jnp.exp(jax.random.uniform(key_frame, (CLIPS, FRAMES), minval=0.0, maxval=math.log(3.4))) / 3.4
    frame_scale = ramp[None, :] * jitter
    chan_scale = jnp.exp(jax.random.uniform(key_chan, (C,), minval=math.log(0.3), maxval=math.log(3.0)))
    noise = jax.random.truncated_normal(key_noise, -4.0, 4.0, shape)
    value = noise * frame_scale[:, :, None, None, None] * chan_scale
    return value.astype(jnp.bfloat16)


def draw_cotangent(key, part):
    base = jax.random.fold_in(key, 7177)
    key_noise, key_frame, key_offset, key_pair = jax.random.split(base, 4)
    shape = (CLIPS, FRAMES, ROWS, COLS, C)
    position = jnp.arange(FRAMES).astype(jnp.float32) / (FRAMES - 1)
    ramp = jnp.exp(math.log(3.0) * position)
    jitter = jnp.exp(jax.random.uniform(key_frame, (CLIPS, FRAMES), minval=math.log(0.5), maxval=0.0))
    frame_scale = ramp[None, :] * jitter
    blocks = FRAMES // F_DEV
    chan_block = C // blocks
    pairing = jax.random.permutation(key_pair, blocks)
    frame_block = jnp.arange(FRAMES) // F_DEV
    chan_owner = jnp.arange(C) // chan_block
    boosted = (pairing[frame_block][:, None] == chan_owner[None, :]).astype(jnp.float32)
    boost = 1.0 + 2.0 * boosted
    offset = jax.random.uniform(key_offset, (C,), minval=-0.5, maxval=0.5)
    noise = jax.random.truncated_normal(key_noise, -4.0, 4.0, shape) + offset
    value = noise * frame_scale[:, :, None, None, None] * boost[None, :, None, None, :]
    return value.astype(jnp.bfloat16)


def levels(stream_key, dims, cuts, smallest, largest):
    gain, own = 1.0, jax.random.fold_in(stream_key, 6)
    for axis_at, parts in cuts:
        draws = jnp.exp(jax.random.uniform(jax.random.fold_in(own, axis_at), (parts,), jnp.float32, smallest / len(cuts), largest / len(cuts)))
        gain = gain * jnp.repeat(draws, dims[axis_at] // parts).reshape([-1 if axis == axis_at else 1 for axis in range(len(dims))])
    return gain


def bell_draw(key, shape, scale, bound, cuts=(), kind=jnp.bfloat16):
    result = jax.random.normal(key, shape, jnp.float32) * scale
    if len(cuts) > 0:
        result = levels(key, shape, cuts, -0.22, 0.18) * result
    return jnp.clip(result, min=-bound, max=bound).astype(kind)


def setup_inputs(seed: int = 0) -> dict:
    splits = jax.random.split(jax.random.key(seed), 7)
    return {
        "latents": draw_latents(jax.random.fold_in(splits[6], 71), 0),
        "cotangent": draw_cotangent(jax.random.fold_in(splits[6], 71), 0),
        "norm_gain": jnp.clip(1.0 + 0.15 * jax.random.normal(splits[2], (C,), jnp.float32), 0.25, 1.75),
        "norm_bias": bell_draw(splits[3], (C,), 0.5, 3.0, (), jnp.float32),
        "w_spatial": bell_draw(splits[4], (9 * C, C), (9 * C) ** -0.5, 0.125, ((0, 8),)),
        "w_temporal": bell_draw(splits[5], (3 * C, C), (3 * C) ** -0.5, 0.21875, ((0, 8),)),
    }


epsilon = 1e-05

def contract(left, right):
    return lax.dot_general(left, right, (((0,), (0,)), ((), ())), preferred_element_type=jnp.float32)

def spatial_forward(activated, weights):
    frames, rows_here, cols_here, channels = activated.shape
    padded = jnp.pad(activated, ((0, 0), (1, 1), (1, 1), (0, 0)))
    running = jnp.zeros((frames * rows_here * cols_here, channels), jnp.float32)
    for tap_row in range(3):
        for tap_col in range(3):
            tap_index = 3 * tap_row + tap_col
            window = padded[:, tap_row:tap_row + rows_here, tap_col:tap_col + cols_here, :].reshape(-1, channels)
            running = running + jnp.dot(window, weights[tap_index * channels:(tap_index + 1) * channels], preferred_element_type=jnp.float32)
    return running.reshape(frames, rows_here, cols_here, channels)

def spatial_backward(activated, grad_out, weights):
    frames, rows_here, cols_here, channels = activated.shape
    pad_act = jnp.pad(activated, ((0, 0), (1, 1), (1, 1), (0, 0)))
    pad_grad = jnp.pad(grad_out, ((0, 0), (1, 1), (1, 1), (0, 0)))
    flat_grad = grad_out.reshape(-1, channels)
    running = jnp.zeros((frames * rows_here * cols_here, channels), jnp.float32)
    pieces = []
    for tap_row in range(3):
        for tap_col in range(3):
            tap_index = 3 * tap_row + tap_col
            block = weights[tap_index * channels:(tap_index + 1) * channels]
            window_grad = pad_grad[:, 2 - tap_row:2 - tap_row + rows_here, 2 - tap_col:2 - tap_col + cols_here, :].reshape(-1, channels)
            running = running + jnp.dot(window_grad, block.T, preferred_element_type=jnp.float32)
            window_act = pad_act[:, tap_row:tap_row + rows_here, tap_col:tap_col + cols_here, :].reshape(-1, channels)
            pieces.append(contract(window_act, flat_grad))
    return (running.reshape(frames, rows_here, cols_here, channels), jnp.concatenate(pieces, axis=0))

def temporal_apply(extended, weights, frames):
    channels = extended.shape[-1]
    shape_out = (extended.shape[0], frames, extended.shape[2], channels)
    running = jnp.zeros((shape_out[0] * frames * shape_out[2], channels), jnp.float32)
    for time_delay in range(3):
        earlier = extended[:, 2 - time_delay:2 - time_delay + frames].reshape(-1, channels)
        running = running + jnp.dot(earlier, weights[time_delay * channels:(time_delay + 1) * channels], preferred_element_type=jnp.float32)
    return running.reshape(shape_out)

def temporal_adjoint(earlier_ext, later_ext, grad_rows, weights):
    frames = grad_rows.shape[1]
    channels = grad_rows.shape[-1]
    flat_grad = grad_rows.reshape(-1, channels)
    running = jnp.zeros(flat_grad.shape, jnp.float32)
    pieces = []
    for time_delay in range(3):
        block = weights[time_delay * channels:(time_delay + 1) * channels]
        later_rows = later_ext[:, time_delay:time_delay + frames].reshape(-1, channels)
        running = running + jnp.dot(later_rows, block.T, preferred_element_type=jnp.float32)
        earlier = earlier_ext[:, 2 - time_delay:2 - time_delay + frames].reshape(-1, channels)
        pieces.append(contract(earlier, flat_grad))
    return (running.reshape(grad_rows.shape), jnp.concatenate(pieces, axis=0))

def clip_pass(latents, cotangent, norm_gain, norm_bias, w_spatial, w_temporal):
    latents = latents[None]
    cotangent = cotangent[None]
    clip_count, frames, rows_here, cols_here, channels = latents.shape
    per_group = channels // GROUPS
    widened = latents.astype(jnp.float32).reshape(clip_count, frames, rows_here, cols_here, GROUPS, per_group)
    cells_count = frames * rows_here * cols_here * per_group
    group_mean = lax.optimization_barrier(jnp.sum(widened, axis=(1, 2, 3, 5))) / cells_count
    variance = lax.optimization_barrier(jnp.sum(widened * widened, axis=(1, 2, 3, 5))) / cells_count - group_mean * group_mean
    inv_std = 1.0 / jnp.sqrt(variance + epsilon)
    mean_wide = group_mean[:, None, None, None, :, None]
    std_wide = inv_std[:, None, None, None, :, None]
    whitened = (widened - mean_wide) * std_wide
    flat_white = whitened.reshape(latents.shape)
    normed = flat_white * norm_gain + norm_bias
    sigmoid = jax.nn.sigmoid(normed)
    activated = (normed * sigmoid).astype(jnp.bfloat16)
    silu_slope = sigmoid * (1.0 + normed * (1.0 - sigmoid))
    cell_count = rows_here * cols_here
    stacked = activated.reshape(clip_count * frames, rows_here, cols_here, channels)
    spatial = spatial_forward(stacked, w_spatial).astype(jnp.bfloat16).reshape(clip_count, frames, cell_count, channels)
    earlier_ext = jnp.pad(spatial, ((0, 0), (2, 0), (0, 0), (0, 0)))
    temporal = temporal_apply(earlier_ext, w_temporal, frames)
    block_out = (latents.astype(jnp.float32) + temporal.reshape(latents.shape)).astype(jnp.bfloat16)
    grad_rows = cotangent.reshape(clip_count, frames, cell_count, channels)
    later_ext = jnp.pad(grad_rows, ((0, 0), (0, 2), (0, 0), (0, 0)))
    grad_wide, grads_temporal = temporal_adjoint(earlier_ext, later_ext, grad_rows, w_temporal)
    grad_spatial_act = grad_wide.astype(jnp.bfloat16).reshape(clip_count * frames, rows_here, cols_here, channels)
    grad_activated, grads_spatial = spatial_backward(stacked, grad_spatial_act, w_spatial)
    grad_normed = grad_activated.reshape(latents.shape) * silu_slope
    gain_term = lax.optimization_barrier(jnp.sum(grad_normed * flat_white, axis=(0, 1, 2, 3)))
    bias_term = lax.optimization_barrier(jnp.sum(grad_normed, axis=(0, 1, 2, 3)))
    grad_white = (grad_normed * norm_gain).reshape(widened.shape)
    grad_mean = lax.optimization_barrier(jnp.sum(grad_white, axis=(1, 2, 3, 5))) / cells_count
    grad_cross = lax.optimization_barrier(jnp.sum(grad_white * whitened, axis=(1, 2, 3, 5))) / cells_count
    inner = (grad_white - grad_mean[:, None, None, None, :, None] - whitened * grad_cross[:, None, None, None, :, None]) * std_wide
    grad_input = (cotangent.astype(jnp.float32) + inner.reshape(latents.shape)).astype(jnp.bfloat16)
    return (block_out[0], grad_input[0], grads_spatial, grads_temporal, jnp.stack([gain_term, bias_term]))

def reference(latents, cotangent, norm_gain, norm_bias, w_spatial, w_temporal):

    def one_clip(clip_pair):
        return clip_pass(clip_pair[0], clip_pair[1], norm_gain, norm_bias, w_spatial, w_temporal)
    results = lax.map(one_clip, (latents, cotangent))
    grad_scale = 1.0 / math.sqrt(CLIPS * FRAMES * ROWS * COLS)
    return (results[0], results[1], lax.optimization_barrier(jnp.sum(results[2], axis=0)) * grad_scale, lax.optimization_barrier(jnp.sum(results[3], axis=0)) * grad_scale, lax.optimization_barrier(jnp.sum(results[4], axis=0)) * grad_scale)
```

```python
import math

import jax
import jax.numpy as jnp
from jax import lax
from jax.experimental import pallas as pl
from jax.experimental.pallas import tpu as pltpu
from jax.sharding import PartitionSpec as P

MESH = pl.DeviceIdType.MESH
F32 = jnp.float32
BF16 = jnp.bfloat16
GROUPS = 32
EPSILON = 1e-05
C = 256
CELLS = 128
COLS = 16
ROWS = 256
NX, NZH, NY, NZL, NC = 4, 2, 4, 8, 2
S_TILE = (0, 4, 9, 13)
T_TILE = (0, 1, 3, 4)
WIN = 7 * 128
ZWIN = 5 * 128


def coords():
    dp, wide = lax.axis_index("dp"), lax.axis_index("wide")
    return (
        lax.div(dp, 2),
        lax.rem(dp, 2),
        lax.div(wide, 16),
        lax.rem(lax.div(wide, 2), 8),
        lax.rem(wide, 2),
    )


def device(x, zh, y, zl, c):
    return (x * 2 + zh, (y * 8 + zl) * 2 + c)


def remote(src, dst, send_sem, recv_sem, target):
    return pltpu.make_async_remote_copy(
        src_ref=src,
        dst_ref=dst,
        send_sem=send_sem,
        recv_sem=recv_sem,
        device_id=target,
        device_id_type=MESH,
    )


def greet(targets):
    barrier = pltpu.get_barrier_semaphore()
    for target in targets:
        pl.semaphore_signal(barrier, inc=1, device_id=target, device_id_type=MESH)
    return lambda: pl.semaphore_wait(barrier, len(targets))


def plane_peers(x, zh, y, zl, c):
    mine = y * 2 + c
    peers = []
    for k in range(1, 8):
        other = lax.rem(mine + k, 8)
        peers.append((other, device(x, zh, lax.div(other, 2), zl, lax.rem(other, 2))))
    return mine, peers


def line_peers(x, zh, y, zl, c):
    peers = []
    for k in range(1, 8):
        other = lax.rem(zl + k, 8)
        peers.append((other, device(x, zh, y, other, c)))
    return zl, peers


class Exchange:
    def __init__(self, slots, send_sem, recv_sem, mine, peers):
        self.copies = []
        self.arrivals = []
        for at, (other, target) in enumerate(peers):
            self.copies.append(
                remote(slots.at[mine], slots.at[mine], send_sem.at[at], recv_sem.at[mine], target)
            )
            self.arrivals.append(
                remote(slots.at[other], slots.at[other], send_sem.at[at], recv_sem.at[other], target)
            )

    def start(self):
        for copy in self.copies:
            copy.start()

    def arrive(self):
        for arrival in self.arrivals:
            arrival.wait_recv()

    def drain(self):
        for copy in self.copies:
            copy.wait_send()


def total(slots, count):
    result = slots[0]
    for k in range(1, count):
        result = result + slots[k]
    return result


def group_ones():
    row = lax.broadcasted_iota(jnp.int32, (C, C), 0)
    col = lax.broadcasted_iota(jnp.int32, (C, C), 1)
    return (lax.div(row, C // GROUPS) == lax.div(col, C // GROUPS)).astype(F32)


def group_totals(two_rows):
    padded = jnp.concatenate([two_rows, jnp.zeros((6, C), F32)], axis=0)
    return jnp.dot(
        padded, group_ones(), precision=lax.Precision.HIGHEST, preferred_element_type=F32
    )


def gather_kernel(
    lat, cot, ws, wt, weights, lat_prev, cot_next, stats,
    plane, line, local_sem, halo_send, halo_recv,
    plane_send, plane_recv, line_send, line_recv,
    x1_send, x1_recv, z_send, z_recv, x2_send, x2_recv,
    y_send, y_recv, c1_send, c1_recv, c2_send, c2_recv,
):
    x, zh, y, zl, c = coords()
    wide = lax.axis_index("wide")
    local_copies = [
        pltpu.make_async_copy(ws, weights.at[zh, x, pl.ds(0, 288)], local_sem.at[0]),
        pltpu.make_async_copy(wt, weights.at[zh, x, pl.ds(288, 96)], local_sem.at[1]),
    ]
    for copy in local_copies:
        copy.start()
    mine, in_plane = plane_peers(x, zh, y, zl, c)
    _, in_line = line_peers(x, zh, y, zl, c)
    after = (lax.axis_index("dp"), lax.rem(wide + 1, 64))
    before = (lax.axis_index("dp"), lax.rem(wide + 63, 64))
    others_x = [lax.rem(x + k, NX) for k in (1, 2, 3)]
    others_y = [lax.rem(y + k, NY) for k in (1, 2, 3)]
    to_x = [device(o, zh, y, zl, c) for o in others_x]
    to_y = [device(x, zh, o, zl, c) for o in others_y]
    to_z = device(x, 1 - zh, y, zl, c)
    to_c = device(x, zh, y, zl, 1 - c)
    arrived = greet(
        [p for _, p in in_plane] + [p for _, p in in_line] + [after, before] + to_x + [to_z]
    )

    wide_lat = lat[...].astype(F32)
    plane[mine, 0:1, :] = jnp.sum(wide_lat, axis=0, keepdims=True)
    plane[mine, 1:2, :] = jnp.sum(wide_lat * wide_lat, axis=0, keepdims=True)
    arrived()

    first = Exchange(plane, plane_send, plane_recv, mine, in_plane)
    first.start()
    for copy in local_copies:
        copy.wait()
    half = pl.multiple_of(c * 192, 16)
    piece = pl.multiple_of(c * 192 + y * 48, 16)
    z_copy = remote(
        weights.at[zh, x, pl.ds(piece, 48)], weights.at[zh, x, pl.ds(piece, 48)],
        z_send.at[0], z_recv.at[0], to_z,
    )
    z_copy.start()
    halo = [
        remote(lat, lat_prev, halo_send.at[0], halo_recv.at[0], after),
        remote(cot, cot_next, halo_send.at[1], halo_recv.at[1], before),
    ]
    for copy in halo:
        copy.start()
    x1 = [
        remote(
            weights.at[zh, x, pl.ds(half, 192)], weights.at[zh, x, pl.ds(half, 192)],
            x1_send.at[k], x1_recv.at[x], to_x[k],
        )
        for k in range(3)
    ]
    for copy in x1:
        copy.start()

    first.arrive()
    line[zl] = total(plane, 8)
    second = Exchange(line, line_send, line_recv, zl, in_line)
    second.start()

    remote(
        weights.at[1 - zh, x, pl.ds(piece, 48)], weights.at[1 - zh, x, pl.ds(piece, 48)],
        z_send.at[0], z_recv.at[0], to_z,
    ).wait_recv()
    x2 = [
        remote(
            weights.at[1 - zh, x, pl.ds(piece, 48)], weights.at[1 - zh, x, pl.ds(piece, 48)],
            x2_send.at[k], x2_recv.at[x], to_x[k],
        )
        for k in range(3)
    ]
    for copy in x2:
        copy.start()

    second.arrive()
    stats[...] = total(line, 8)

    for k in range(3):
        o = others_x[k]
        part = weights.at[1 - zh, o, pl.ds(piece, 48)]
        remote(part, part, x2_send.at[k], x2_recv.at[o], to_x[k]).wait_recv()
    spread = weights.at[1 - zh, :, pl.ds(piece, 48)]
    ys = [remote(spread, spread, y_send.at[k], y_recv.at[y], to_y[k]) for k in range(3)]
    for copy in ys:
        copy.start()
    c1 = []
    for k in range(3):
        o = others_x[k]
        part = weights.at[zh, o, pl.ds(half, 192)]
        remote(part, part, x1_send.at[k], x1_recv.at[o], to_x[k]).wait_recv()
        copy = remote(part, part, c1_send.at[k], c1_recv.at[k], to_c)
        copy.start()
        c1.append(copy)
    for k in range(3):
        o = others_y[k]
        their_piece = pl.multiple_of(c * 192 + o * 48, 16)
        part = weights.at[1 - zh, :, pl.ds(their_piece, 48)]
        remote(part, part, y_send.at[k], y_recv.at[o], to_y[k]).wait_recv()
    part = weights.at[1 - zh, :, pl.ds(half, 192)]
    c2 = remote(part, part, c2_send.at[0], c2_recv.at[0], to_c)
    c2.start()

    other_half = pl.multiple_of((1 - c) * 192, 16)
    for k in range(3):
        part = weights.at[zh, others_x[k], pl.ds(other_half, 192)]
        remote(part, part, c1_send.at[k], c1_recv.at[k], to_c).wait_recv()
    part = weights.at[1 - zh, :, pl.ds(other_half, 192)]
    remote(part, part, c2_send.at[0], c2_recv.at[0], to_c).wait_recv()
    for copy in halo:
        copy.wait_recv()
    first.drain()
    second.drain()
    for copy in halo + x1 + [z_copy] + x2 + ys + c1 + [c2]:
        copy.wait_send()


def gather(lat, cot, ws, wt):
    vmem = pl.BlockSpec(memory_space=pltpu.VMEM)
    dma = pltpu.SemaphoreType.DMA
    return pl.pallas_call(
        gather_kernel,
        name="gather",
        out_shape=(
            jax.ShapeDtypeStruct((NZH, NX, 384, C), BF16),
            jax.ShapeDtypeStruct((ROWS, C), BF16),
            jax.ShapeDtypeStruct((ROWS, C), BF16),
            jax.ShapeDtypeStruct((2, C), F32),
        ),
        in_specs=[vmem] * 4,
        out_specs=(vmem,) * 4,
        scratch_shapes=[
            pltpu.VMEM((8, 2, C), F32),
            pltpu.VMEM((8, 2, C), F32),
            dma((2,)), dma((2,)), dma((2,)),
            dma((7,)), dma((8,)), dma((7,)), dma((8,)),
            dma((3,)), dma((4,)), dma((1,)), dma((1,)), dma((3,)), dma((4,)),
            dma((3,)), dma((4,)), dma((3,)), dma((3,)), dma((1,)), dma((1,)),
        ],
        compiler_params=pltpu.CompilerParams(
            collective_id=1, has_side_effects=True, vmem_limit_bytes=32 << 20
        ),
    )(lat, cot, ws, wt)


def column_iota(rows):
    return lax.rem(lax.broadcasted_iota(jnp.int32, (rows, C), 0), COLS)


def shifted(values, step):
    rows = values.shape[0]
    if step == 0:
        return values.astype(BF16)
    col = column_iota(rows)
    moved = pltpu.roll(values, (rows - step) % rows, 0)
    edge = COLS - 1 if step == 1 else 0
    return jnp.where(col == edge, 0.0, moved).astype(BF16)


def fill_windows(target, values, sign):
    frames = values.shape[0] // CELLS
    for dx in range(3):
        cols = shifted(values, sign * (dx - 1))
        for dy in range(3):
            step = sign * (dy - 1)
            lanes = pl.ds((3 * dy + dx) * C, C)
            if step == 0:
                target[:, lanes] = cols
                continue
            for frame in range(frames):
                base = frame * CELLS
                if step == 1:
                    target[base : base + CELLS - COLS, lanes] = cols[base + COLS : base + CELLS]
                    target[base + CELLS - COLS : base + CELLS, lanes] = jnp.zeros((COLS, C), BF16)
                else:
                    target[base + COLS : base + CELLS, lanes] = cols[base : base + CELLS - COLS]
                    target[base : base + COLS, lanes] = jnp.zeros((COLS, C), BF16)


def permutation():
    row = lax.broadcasted_iota(jnp.int32, (C, C), 0)
    col = lax.broadcasted_iota(jnp.int32, (C, C), 1)
    j = lax.rem(row, 4)
    zl = lax.rem(lax.div(row, 4), 4) + 4 * lax.rem(lax.div(row, 64), 2)
    y = lax.rem(lax.div(row, 16), 4)
    c = lax.div(row, 128)
    return (col == y * 64 + zl * 8 + c * 4 + j).astype(F32).astype(BF16)


def times_transpose(left, right):
    return lax.dot_general(left, right, (((1,), (1,)), ((), ())), preferred_element_type=F32)


def block_kernel(
    lat, cot, lat_prev, cot_next, stats, gain, bias, weights,
    block_out, grads, norm_sums, grad_white, white, inverse,
    windows, spatial, mixed, adjoint, w_sp, w_tm,
):
    wide = lax.axis_index("wide")
    for d in range(8):
        w_sp[d * 288 : (d + 1) * 288, :] = weights[d % 2, d // 2, 0:288, :]
        w_tm[d * 96 : (d + 1) * 96, :] = weights[d % 2, d // 2, 288:384, :]
    sums = group_totals(stats[...]) / (FRAMES_CELLS * (C // GROUPS))
    mean = sums[0:1]
    inv = 1.0 / jnp.sqrt(sums[1:2] - mean * mean + EPSILON)
    inverse[...] = inv
    gains, biases = gain[...], bias[...]

    def normed_of(values):
        whitened = (values.astype(F32) - mean) * inv
        return whitened, whitened * gains + biases

    whitened, normed = normed_of(lat[...])
    white[...] = whitened
    sigmoid = jax.nn.sigmoid(normed)
    slope = sigmoid * (1.0 + normed * (1.0 - sigmoid))
    _, before = normed_of(lat_prev[...])
    fill_windows(windows.at[ROWS:, :], normed * sigmoid, 1)
    fill_windows(windows.at[:ROWS, :], before * jax.nn.sigmoid(before), 1)
    conv = jnp.dot(windows[...], w_sp[...], preferred_element_type=F32)
    spatial[ROWS:, :] = conv[ROWS:].astype(BF16)
    spatial[:ROWS, :] = jnp.where(wide > 0, conv[:ROWS], 0.0).astype(BF16)
    for delay in range(3):
        start = (2 - delay) * CELLS
        mixed[:, delay * C : (delay + 1) * C] = spatial[start : start + ROWS, :]
    temporal = jnp.dot(mixed[...], w_tm[...], preferred_element_type=F32)
    block_out[...] = (lat[...].astype(F32) + temporal).astype(BF16)

    later = jnp.where(wide < 63, cot_next[...].astype(F32), 0.0).astype(BF16)
    own = cot[...]
    shifts = (own, jnp.concatenate([own[CELLS:], later[:CELLS]], axis=0), later)
    running = jnp.zeros((ROWS, C), F32)
    for delay in range(3):
        running = running + times_transpose(shifts[delay], w_tm[delay * C : (delay + 1) * C, :])
    grad_act = running.astype(BF16)
    fill_windows(adjoint, grad_act.astype(F32), -1)
    running = jnp.zeros((ROWS, C), F32)
    for tap in range(9):
        lanes = slice(tap * C, (tap + 1) * C)
        running = running + times_transpose(adjoint[:, lanes], w_sp[lanes, :])
    grad_normed = running * slope
    norm_sums[0:1, :] = jnp.sum(grad_normed * whitened, axis=0, keepdims=True)
    norm_sums[1:2, :] = jnp.sum(grad_normed, axis=0, keepdims=True)
    grad_white[...] = grad_normed * gains

    order = permutation()
    act_t = times_transpose(order, grad_act).astype(BF16)
    cot_t = times_transpose(order, own).astype(BF16)
    grads[:, : 9 * C] = jnp.dot(
        act_t, windows[ROWS:, :], preferred_element_type=F32
    ).astype(BF16)
    grads[:, 9 * C :] = jnp.dot(cot_t, mixed[...], preferred_element_type=F32).astype(BF16)


FRAMES_CELLS = 128 * CELLS


def block(lat, cot, lat_prev, cot_next, stats, gain, bias, weights):
    vmem = pl.BlockSpec(memory_space=pltpu.VMEM)
    return pl.pallas_call(
        block_kernel,
        name="block",
        out_shape=(
            jax.ShapeDtypeStruct((ROWS, C), BF16),
            jax.ShapeDtypeStruct((C, 12 * C), BF16),
            jax.ShapeDtypeStruct((2, C), F32),
            jax.ShapeDtypeStruct((ROWS, C), F32),
            jax.ShapeDtypeStruct((ROWS, C), F32),
            jax.ShapeDtypeStruct((1, C), F32),
        ),
        in_specs=[vmem] * 8,
        out_specs=(vmem,) * 6,
        scratch_shapes=[
            pltpu.VMEM((2 * ROWS, 9 * C), BF16),
            pltpu.VMEM((2 * ROWS, C), BF16),
            pltpu.VMEM((ROWS, 3 * C), BF16),
            pltpu.VMEM((ROWS, 9 * C), BF16),
            pltpu.VMEM((9 * C, C), BF16),
            pltpu.VMEM((3 * C, C), BF16),
        ],
        compiler_params=pltpu.CompilerParams(vmem_limit_bytes=48 << 20),
    )(lat, cot, lat_prev, cot_next, stats, gain, bias, weights)


def windows_of(values, which):
    s, t = S_TILE[which] * 128, (18 + T_TILE[which]) * 128
    return values[:, s : s + 640], values[:, t : t + 256]


def reduce_kernel(
    grads, norm_sums, grad_white, white, inverse, gain, cot,
    grad_latents, grad_sums, grad_norm,
    plane, line, chips, core_in, a1, b1, a1_in, b1_in, a2, b2, a2_in, b2_in, z1, z_in,
    plane_send, plane_recv, line_send, line_recv, chip_send, chip_recv,
    core_send, core_recv, a1_send, a1_recv, b1_send, b1_recv,
    a2_send, a2_recv, b2_send, b2_recv, zs_send, zs_recv,
):
    x, zh, y, zl, c = coords()
    wide, dp = lax.axis_index("wide"), lax.axis_index("dp")
    mine, in_plane = plane_peers(x, zh, y, zl, c)
    _, in_line = line_peers(x, zh, y, zl, c)
    others_x = [lax.rem(x + k, NX) for k in (1, 2, 3)]
    others_y = [lax.rem(y + k, NY) for k in (1, 2, 3)]
    to_x = [device(o, zh, y, zl, c) for o in others_x]
    to_y = [device(x, zh, o, zl, c) for o in others_y]
    to_c = device(x, zh, y, zl, 1 - c)
    others_dp = [lax.rem(dp + k, 8) for k in range(1, 8)]
    to_dp = [(o, wide) for o in others_dp]
    at_z = zh * 8 + zl
    others_z = [lax.rem(at_z + k, 16) for k in range(1, 16)]
    to_z = [device(x, lax.div(o, 8), y, lax.rem(o, 8), c) for o in others_z]
    arrived = greet([p for _, p in in_plane] + to_dp + to_z)
    plane[mine] = norm_sums[...]
    arrived()

    away = pl.multiple_of((1 - c) * 128, 128)
    core = remote(grads.at[pl.ds(away, 128)], core_in, core_send.at[0], core_recv.at[0], to_c)
    first = Exchange(plane, plane_send, plane_recv, mine, in_plane)
    first.start()
    core.start()
    first.arrive()
    line[zl] = total(plane, 8)
    second = Exchange(line, line_send, line_recv, zl, in_line)
    second.start()

    core.wait_recv()
    for o in range(NY):
        rows = pl.ds(pl.multiple_of(c * 128 + o * 16, 16), 16)
        a1[o] = (
            grads[rows, :].astype(F32) + core_in[o * 16 : (o + 1) * 16, :].astype(F32)
        ).astype(BF16)
    step_a1 = [
        remote(a1.at[others_y[k]], a1_in.at[y], a1_send.at[k], a1_recv.at[y], to_y[k])
        for k in range(3)
    ]
    for copy in step_a1:
        copy.start()
    rows = pl.ds(pl.multiple_of(c * 128 + 64, 16), 64)
    for o in range(NX):
        s, t = S_TILE[o] * 128, (18 + T_TILE[o]) * 128
        for start, width, put in ((s, 640, 0), (t, 256, 640)):
            b1[o, :, put : put + width] = (
                grads[rows, start : start + width].astype(F32)
                + core_in[64:128, start : start + width].astype(F32)
            ).astype(BF16)
    step_b1 = [
        remote(b1.at[others_x[k]], b1_in.at[x], b1_send.at[k], b1_recv.at[x], to_x[k])
        for k in range(3)
    ]
    for copy in step_b1:
        copy.start()

    second.arrive()
    sums = total(line, 8)
    chips[dp] = sums
    step_dp = [
        remote(chips.at[dp], chips.at[dp], chip_send.at[k], chip_recv.at[dp], to_dp[k])
        for k in range(7)
    ]
    for copy in step_dp:
        copy.start()
    means = group_totals(sums * gain[...]) / (FRAMES_CELLS * (C // GROUPS))
    inner = (grad_white[...] - means[1:2] - white[...] * means[0:1]) * inverse[...]
    grad_latents[...] = (cot[...].astype(F32) + inner).astype(BF16)

    for k in range(3):
        o = others_y[k]
        remote(a1.at[o], a1_in.at[o], a1_send.at[k], a1_recv.at[o], to_y[k]).wait_recv()
    joined = a1[y].astype(F32)
    for k in range(3):
        joined = joined + a1_in[others_y[k]].astype(F32)
    joined = joined.astype(BF16)
    for o in range(NX):
        s, t = windows_of(joined, o)
        a2[o, :, 0:640] = s
        a2[o, :, 640:WIN] = t
    step_a2 = [
        remote(a2.at[others_x[k]], a2_in.at[x], a2_send.at[k], a2_recv.at[x], to_x[k])
        for k in range(3)
    ]
    for copy in step_a2:
        copy.start()
    for k in range(3):
        o = others_x[k]
        remote(b1.at[o], b1_in.at[o], b1_send.at[k], b1_recv.at[o], to_x[k]).wait_recv()
    joined = b1[x].astype(F32)
    for k in range(3):
        joined = joined + b1_in[others_x[k]].astype(F32)
    joined = joined.astype(BF16)
    for o in range(NY):
        b2[o] = joined[o * 16 : (o + 1) * 16, :]
    step_b2 = [
        remote(b2.at[others_y[k]], b2_in.at[y], b2_send.at[k], b2_recv.at[y], to_y[k])
        for k in range(3)
    ]
    for copy in step_b2:
        copy.start()

    for k in range(3):
        o = others_x[k]
        remote(a2.at[o], a2_in.at[o], a2_send.at[k], a2_recv.at[o], to_x[k]).wait_recv()
    half_a = a2[x].astype(F32)
    for k in range(3):
        half_a = half_a + a2_in[others_x[k]].astype(F32)
    for k in range(3):
        o = others_y[k]
        remote(b2.at[o], b2_in.at[o], b2_send.at[k], b2_recv.at[o], to_y[k]).wait_recv()
    half_b = b2[y].astype(F32)
    for k in range(3):
        half_b = half_b + b2_in[others_y[k]].astype(F32)
    for h, part in enumerate((half_a, half_b)):
        for q in range(4):
            four = part[q * 4 : (q + 1) * 4, :]
            for hi in range(NZH):
                z1[hi * 8 + h * 4 + q, :, 0:384] = four[:, hi * 256 : hi * 256 + 384].astype(z1.dtype)
                z1[hi * 8 + h * 4 + q, :, 384:ZWIN] = four[:, 640:WIN].astype(z1.dtype)
    step_z = [
        remote(z1.at[others_z[k]], z_in.at[at_z], zs_send.at[k], zs_recv.at[at_z], to_z[k])
        for k in range(15)
    ]
    for copy in step_z:
        copy.start()

    scale = 1.0 / math.sqrt(131072)
    for k in range(7):
        o = others_dp[k]
        remote(chips.at[o], chips.at[o], chip_send.at[k], chip_recv.at[o], to_dp[k]).wait_recv()
    grad_norm[...] = total(chips, 8) * scale
    for k in range(15):
        o = others_z[k]
        remote(z1.at[o], z_in.at[o], zs_send.at[k], zs_recv.at[o], to_z[k]).wait_recv()
    result = z1[at_z].astype(F32)
    for k in range(15):
        result = result + z_in[others_z[k]].astype(F32)
    grad_sums[...] = result * scale
    first.drain()
    second.drain()
    for copy in [core] + step_a1 + step_b1 + step_dp + step_a2 + step_b2 + step_z:
        copy.wait_send()


Z_TYPE = BF16


def reduce(grads, norm_sums, grad_white, white, inverse, gain, cot):
    vmem = pl.BlockSpec(memory_space=pltpu.VMEM)
    dma = pltpu.SemaphoreType.DMA
    return pl.pallas_call(
        reduce_kernel,
        name="reduce",
        out_shape=(
            jax.ShapeDtypeStruct((ROWS, C), BF16),
            jax.ShapeDtypeStruct((4, ZWIN), F32),
            jax.ShapeDtypeStruct((2, C), F32),
        ),
        in_specs=[vmem] * 7,
        out_specs=(vmem,) * 3,
        scratch_shapes=[
            pltpu.VMEM((8, 2, C), F32),
            pltpu.VMEM((8, 2, C), F32),
            pltpu.VMEM((8, 2, C), F32),
            pltpu.VMEM((128, 12 * C), BF16),
            pltpu.VMEM((NY, 16, 12 * C), BF16),
            pltpu.VMEM((NX, 64, WIN), BF16),
            pltpu.VMEM((NY, 16, 12 * C), BF16),
            pltpu.VMEM((NX, 64, WIN), BF16),
            pltpu.VMEM((NX, 16, WIN), BF16),
            pltpu.VMEM((NY, 16, WIN), BF16),
            pltpu.VMEM((NX, 16, WIN), BF16),
            pltpu.VMEM((NY, 16, WIN), BF16),
            pltpu.VMEM((16, 4, ZWIN), Z_TYPE),
            pltpu.VMEM((16, 4, ZWIN), Z_TYPE),
            dma((7,)), dma((8,)), dma((7,)), dma((8,)), dma((7,)), dma((8,)),
            dma((1,)), dma((1,)), dma((3,)), dma((4,)), dma((3,)), dma((4,)),
            dma((3,)), dma((4,)), dma((3,)), dma((4,)), dma((15,)), dma((16,)),
        ],
        compiler_params=pltpu.CompilerParams(
            collective_id=2, has_side_effects=True, vmem_limit_bytes=48 << 20
        ),
    )(grads, norm_sums, grad_white, white, inverse, gain, cot)


def local(latents, cotangent, norm_gain, norm_bias, w_spatial, w_temporal):
    lat, cot = latents.reshape(ROWS, C), cotangent.reshape(ROWS, C)
    gain, bias = norm_gain.reshape(1, C), norm_bias.reshape(1, C)
    weights, lat_prev, cot_next, stats = gather(lat, cot, w_spatial, w_temporal)
    block_out, grads, norm_sums, grad_white, white, inverse = block(
        lat, cot, lat_prev, cot_next, stats, gain, bias, weights
    )
    grad_latents, grad_sums, grad_norm = reduce(
        grads, norm_sums, grad_white, white, inverse, gain, cot
    )
    dp, wide = lax.axis_index("dp"), lax.axis_index("wide")
    odd, hi = lax.rem(lax.div(dp, 2), 2), lax.rem(dp, 2)
    spatial = lax.dynamic_slice(grad_sums[:, :384], (0, 64 * odd + 32 * hi), (4, 288))
    temporal = lax.dynamic_slice(grad_sums[:, 384:], (0, 64 * odd + 96 * hi), (4, 96))
    return (
        block_out.reshape(latents.shape),
        grad_latents.reshape(latents.shape),
        spatial.T,
        temporal.T,
        lax.dynamic_slice(grad_norm, (0, 4 * wide), (2, 4)),
    )


def solution(mesh):
    return jax.shard_map(
        local,
        mesh=mesh,
        in_specs=(
            P("dp", "wide", None, None, None),
            P("dp", "wide", None, None, None),
            P(),
            P(),
            P("dp", None),
            P("dp", None),
        ),
        out_specs=(
            P("dp", "wide", None, None, None),
            P("dp", "wide", None, None, None),
            P("dp", "wide"),
            P("dp", "wide"),
            P(None, "wide"),
        ),
        check_vma=False,
    )
```

```python
import math

import jax
import jax.numpy as jnp
from jax import lax
from jax.experimental import pallas as pl
from jax.experimental.pallas import tpu as pltpu
from jax.sharding import PartitionSpec as P

MESH = pl.DeviceIdType.MESH
F32 = jnp.float32
BF16 = jnp.bfloat16
GROUPS = 32
EPSILON = 1e-05
C = 256
CELLS = 128
COLS = 16
ROWS = 256
NX, NZH, NY, NZL, NC = 4, 2, 4, 8, 2
S_TILE = (0, 4, 9, 13)
T_TILE = (0, 1, 3, 4)
WIN = 7 * 128
ZWIN = 5 * 128


def coords():
    dp, wide = lax.axis_index("dp"), lax.axis_index("wide")
    return (
        lax.div(dp, 2),
        lax.rem(dp, 2),
        lax.div(wide, 16),
        lax.rem(lax.div(wide, 2), 8),
        lax.rem(wide, 2),
    )


def device(x, zh, y, zl, c):
    return (x * 2 + zh, (y * 8 + zl) * 2 + c)


def remote(src, dst, send_sem, recv_sem, target):
    return pltpu.make_async_remote_copy(
        src_ref=src,
        dst_ref=dst,
        send_sem=send_sem,
        recv_sem=recv_sem,
        device_id=target,
        device_id_type=MESH,
    )


def greet(targets):
    barrier = pltpu.get_barrier_semaphore()
    for target in targets:
        pl.semaphore_signal(barrier, inc=1, device_id=target, device_id_type=MESH)
    return lambda: pl.semaphore_wait(barrier, len(targets))


def plane_peers(x, zh, y, zl, c):
    mine = y * 2 + c
    peers = []
    for k in range(1, 8):
        other = lax.rem(mine + k, 8)
        peers.append((other, device(x, zh, lax.div(other, 2), zl, lax.rem(other, 2))))
    return mine, peers


def line_peers(x, zh, y, zl, c):
    peers = []
    for k in range(1, 8):
        other = lax.rem(zl + k, 8)
        peers.append((other, device(x, zh, y, other, c)))
    return zl, peers


def total(slots, count):
    result = slots[0]
    for k in range(1, count):
        result = result + slots[k]
    return result


def group_ones():
    row = lax.broadcasted_iota(jnp.int32, (C, C), 0)
    col = lax.broadcasted_iota(jnp.int32, (C, C), 1)
    return (lax.div(row, C // GROUPS) == lax.div(col, C // GROUPS)).astype(F32)


def group_totals(two_rows):
    padded = jnp.concatenate([two_rows, jnp.zeros((6, C), F32)], axis=0)
    return jnp.dot(
        padded, group_ones(), precision=lax.Precision.HIGHEST, preferred_element_type=F32
    )


def column_iota(rows):
    return lax.rem(lax.broadcasted_iota(jnp.int32, (rows, C), 0), COLS)


def shifted(values, step):
    rows = values.shape[0]
    if step == 0:
        return values.astype(BF16)
    col = column_iota(rows)
    moved = pltpu.roll(values, (rows - step) % rows, 0)
    edge = COLS - 1 if step == 1 else 0
    return jnp.where(col == edge, 0.0, moved).astype(BF16)


def fill_windows(target, values, sign):
    frames = values.shape[0] // CELLS
    for dx in range(3):
        cols = shifted(values, sign * (dx - 1))
        for dy in range(3):
            step = sign * (dy - 1)
            lanes = pl.ds((3 * dy + dx) * C, C)
            if step == 0:
                target[:, lanes] = cols
                continue
            for frame in range(frames):
                base = frame * CELLS
                if step == 1:
                    target[base : base + CELLS - COLS, lanes] = cols[base + COLS : base + CELLS]
                    target[base + CELLS - COLS : base + CELLS, lanes] = jnp.zeros((COLS, C), BF16)
                else:
                    target[base + COLS : base + CELLS, lanes] = cols[base : base + CELLS - COLS]
                    target[base : base + COLS, lanes] = jnp.zeros((COLS, C), BF16)


def permutation():
    row = lax.broadcasted_iota(jnp.int32, (C, C), 0)
    col = lax.broadcasted_iota(jnp.int32, (C, C), 1)
    j = lax.rem(row, 4)
    zl = lax.rem(lax.div(row, 4), 4) + 4 * lax.rem(lax.div(row, 64), 2)
    y = lax.rem(lax.div(row, 16), 4)
    c = lax.div(row, 128)
    return (col == y * 64 + zl * 8 + c * 4 + j).astype(F32).astype(BF16)


def times_transpose(left, right):
    return lax.dot_general(left, right, (((1,), (1,)), ((), ())), preferred_element_type=F32)


FRAMES_CELLS = 128 * CELLS


def windows_of(values, which):
    s, t = S_TILE[which] * 128, (18 + T_TILE[which]) * 128
    return values[:, s : s + 640], values[:, t : t + 256]


SENDS = 96
VMEM_BYTES = 62 << 20


def main_kernel(
    lat_hbm, cot_hbm, ws_hbm, wt_hbm, gain_hbm, bias_hbm,
    out_hbm, latents_hbm, sums_hbm, norm_hbm,
    block_out, grad_latents, grad_sums, grad_norm, lat, cot, gain, bias, lat_prev, cot_next, weights,
    plane, line, plane_b, line_b, pair_b, row_b,
    w_sp, w_tm, windows, spatial, mixed, adjoint, act_t, cot_t,
    away, own, core_in, a1, b1, a1_in, b1_in, a2, b2, a2_in, b2_in, z1, z_in,
    local_sem, store_sem, send_sem,
    plane_recv, line_recv, plane_b_recv, line_b_recv, pair_b_recv, row_b_recv,
    halo_recv, x1_recv, z_recv, x2_recv, y_recv, c1_recv, c2_recv,
    core_recv, a1_recv, b1_recv, a2_recv, b2_recv, zs_recv,
):
    x, zh, y, zl, c = coords()
    wide, dp = lax.axis_index("wide"), lax.axis_index("dp")
    loads = [
        pltpu.make_async_copy(source, target, local_sem.at[k])
        for k, (source, target) in enumerate(
            (
                (lat_hbm, lat),
                (ws_hbm, weights.at[zh, x, pl.ds(0, 288)]),
                (wt_hbm, weights.at[zh, x, pl.ds(288, 96)]),
                (cot_hbm, cot),
                (gain_hbm, gain),
                (bias_hbm, bias),
            )
        )
    ]
    for copy in loads:
        copy.start()
    mine, in_plane = plane_peers(x, zh, y, zl, c)
    _, in_line = line_peers(x, zh, y, zl, c)
    after = (dp, lax.rem(wide + 1, 64))
    before = (dp, lax.rem(wide + 63, 64))
    others_x = [lax.rem(x + k, NX) for k in (1, 2, 3)]
    others_y = [lax.rem(y + k, NY) for k in (1, 2, 3)]
    to_x = [device(o, zh, y, zl, c) for o in others_x]
    to_y = [device(x, zh, o, zl, c) for o in others_y]
    to_c = device(x, zh, y, zl, 1 - c)
    to_far = device(x, 1 - zh, y, lax.rem(zl + 4, 8), c)
    at_z = zh * 8 + zl
    others_z = [lax.rem(at_z + k, 16) for k in range(1, 16)]
    to_z = [device(x, lax.div(o, 8), y, lax.rem(o, 8), c) for o in others_z]
    arrived = greet([p for _, p in in_plane] + [after, before] + to_x + to_z)

    stores = []

    def store(source, target):
        copy = pltpu.make_async_copy(source, target, store_sem.at[len(stores)])
        copy.start()
        stores.append(copy)

    pending = []
    counter = [0]

    def send(source, target, recv, where):
        copy = remote(source, target, send_sem.at[counter[0]], recv, where)
        counter[0] += 1
        copy.start()
        pending.append(copy)

    def receive(ref, recv):
        remote(ref, ref, send_sem.at[0], recv, to_c).wait_recv()

    def exchange(slots, recv, at, peers):
        for _, target in peers:
            send(slots.at[at], slots.at[at], recv.at[at], target)

    def gathered(slots, recv, peers):
        for other, _ in peers:
            receive(slots.at[other], recv.at[other])

    loads[0].wait()
    wide_lat = lat[...].astype(F32)
    plane[mine, 0:1, :] = jnp.sum(wide_lat, axis=0, keepdims=True)
    plane[mine, 1:2, :] = jnp.sum(wide_lat * wide_lat, axis=0, keepdims=True)
    for copy in loads[1:]:
        copy.wait()
    arrived()

    exchange(plane, plane_recv, mine, in_plane)
    half = pl.multiple_of(c * 192, 16)
    other_half = pl.multiple_of((1 - c) * 192, 16)
    piece = pl.multiple_of(c * 192 + y * 48, 16)
    part = weights.at[zh, x, pl.ds(piece, 48)]
    send(part, part, z_recv.at[0], to_far)
    part = weights.at[zh, x, pl.ds(half, 192)]
    for target in to_x:
        send(part, part, x1_recv.at[x], target)
    send(lat, lat_prev, halo_recv.at[0], after)
    send(cot, cot_next, halo_recv.at[1], before)

    gathered(plane, plane_recv, in_plane)
    line[zl] = total(plane, 8)
    exchange(line, line_recv, zl, in_line)

    part = weights.at[1 - zh, x, pl.ds(piece, 48)]
    receive(part, z_recv.at[0])
    for target in to_x:
        send(part, part, x2_recv.at[x], target)
    for o in others_x:
        part = weights.at[zh, o, pl.ds(half, 192)]
        receive(part, x1_recv.at[o])
        send(part, part, c1_recv.at[o], to_c)
    for o in others_x:
        receive(weights.at[1 - zh, o, pl.ds(piece, 48)], x2_recv.at[o])
    part = weights.at[1 - zh, :, pl.ds(piece, 48)]
    for target in to_y:
        send(part, part, y_recv.at[y], target)

    gathered(line, line_recv, in_line)
    sums = group_totals(total(line, 8)) / (FRAMES_CELLS * (C // GROUPS))
    mean = sums[0:1]
    inv = 1.0 / jnp.sqrt(sums[1:2] - mean * mean + EPSILON)
    gains, biases = gain[...], bias[...]

    def normed_of(values):
        whitened = (values.astype(F32) - mean) * inv
        return whitened, whitened * gains + biases

    whitened, normed = normed_of(lat[...])
    fill_windows(windows.at[ROWS:, :], normed * jax.nn.sigmoid(normed), 1)
    receive(lat_prev, halo_recv.at[0])
    _, earlier = normed_of(lat_prev[...])
    fill_windows(windows.at[:ROWS, :], earlier * jax.nn.sigmoid(earlier), 1)
    order = permutation()
    cot_t[...] = times_transpose(order, cot[...]).astype(BF16)

    for o in others_y:
        their_piece = pl.multiple_of(c * 192 + o * 48, 16)
        receive(weights.at[1 - zh, :, pl.ds(their_piece, 48)], y_recv.at[o])
    part = weights.at[1 - zh, :, pl.ds(half, 192)]
    send(part, part, c2_recv.at[0], to_c)
    receive(cot_next, halo_recv.at[1])
    for o in others_x:
        receive(weights.at[zh, o, pl.ds(other_half, 192)], c1_recv.at[o])
    receive(weights.at[1 - zh, :, pl.ds(other_half, 192)], c2_recv.at[0])

    for d in range(8):
        w_sp[d * 288 : (d + 1) * 288, :] = weights[d % 2, d // 2, 0:288, :]
        w_tm[d * 96 : (d + 1) * 96, :] = weights[d % 2, d // 2, 288:384, :]

    later = jnp.where(wide < 63, cot_next[...].astype(F32), 0.0).astype(BF16)
    held = cot[...]
    shifts = (held, jnp.concatenate([held[CELLS:], later[:CELLS]], axis=0), later)
    running = jnp.zeros((ROWS, C), F32)
    for delay in range(3):
        running = running + times_transpose(shifts[delay], w_tm[delay * C : (delay + 1) * C, :])
    grad_act = running.astype(BF16)
    act_t[...] = times_transpose(order, grad_act).astype(BF16)

    theirs = pl.ds(pl.multiple_of((1 - c) * 128, 128), 128)
    ours = pl.ds(pl.multiple_of(c * 128, 128), 128)
    away[0:128, : 9 * C] = jnp.dot(
        act_t[theirs, :], windows[ROWS:, :], preferred_element_type=F32
    ).astype(BF16)
    send(away.at[:, pl.ds(0, 9 * C)], core_in.at[:, pl.ds(0, 9 * C)], core_recv.at[0], to_c)

    conv = jnp.dot(windows[...], w_sp[...], preferred_element_type=F32)
    spatial[ROWS:, :] = conv[ROWS:].astype(BF16)
    spatial[:ROWS, :] = jnp.where(wide > 0, conv[:ROWS], 0.0).astype(BF16)
    for delay in range(3):
        start = (2 - delay) * CELLS
        mixed[:, delay * C : (delay + 1) * C] = spatial[start : start + ROWS, :]
    away[:, 9 * C :] = jnp.dot(
        cot_t[theirs, :], mixed[...], preferred_element_type=F32
    ).astype(BF16)
    send(away.at[:, pl.ds(9 * C, 3 * C)], core_in.at[:, pl.ds(9 * C, 3 * C)], core_recv.at[1], to_c)

    own[:, : 9 * C] = jnp.dot(act_t[ours, :], windows[ROWS:, :], preferred_element_type=F32)
    own[:, 9 * C :] = jnp.dot(cot_t[ours, :], mixed[...], preferred_element_type=F32)

    receive(core_in.at[:, pl.ds(0, 9 * C)], core_recv.at[0])
    receive(core_in.at[:, pl.ds(9 * C, 3 * C)], core_recv.at[1])
    for o in range(NY):
        rows = slice(o * 16, (o + 1) * 16)
        a1[o] = (own[rows, :] + core_in[rows, :].astype(F32)).astype(BF16)
    for o, target in zip(others_y, to_y):
        send(a1.at[o], a1_in.at[y], a1_recv.at[y], target)
    for o in range(NX):
        s, t = S_TILE[o] * 128, (18 + T_TILE[o]) * 128
        for start, width, put in ((s, 640, 0), (t, 256, 640)):
            lanes = slice(start, start + width)
            b1[o, :, put : put + width] = (
                own[64:128, lanes] + core_in[64:128, lanes].astype(F32)
            ).astype(BF16)
    for o, target in zip(others_x, to_x):
        send(b1.at[o], b1_in.at[x], b1_recv.at[x], target)

    fill_windows(adjoint, grad_act.astype(F32), -1)
    running = jnp.zeros((ROWS, C), F32)
    for tap in range(9):
        lanes = slice(tap * C, (tap + 1) * C)
        running = running + times_transpose(adjoint[:, lanes], w_sp[lanes, :])
    sigmoid = jax.nn.sigmoid(normed)
    grad_normed = running * (sigmoid * (1.0 + normed * (1.0 - sigmoid)))
    plane_b[mine, 0:1, :] = jnp.sum(grad_normed * whitened, axis=0, keepdims=True)
    plane_b[mine, 1:2, :] = jnp.sum(grad_normed, axis=0, keepdims=True)
    exchange(plane_b, plane_b_recv, mine, in_plane)
    grad_white = grad_normed * gains

    temporal = jnp.dot(mixed[...], w_tm[...], preferred_element_type=F32)
    block_out[...] = (lat[...].astype(F32) + temporal).astype(BF16)
    store(block_out, out_hbm)

    gathered(plane_b, plane_b_recv, in_plane)
    line_b[zl] = total(plane_b, 8)
    exchange(line_b, line_b_recv, zl, in_line)

    for o in others_y:
        receive(a1_in.at[o], a1_recv.at[o])
    joined = a1[y].astype(F32)
    for o in others_y:
        joined = joined + a1_in[o].astype(F32)
    joined = joined.astype(BF16)
    for o in range(NX):
        s, t = windows_of(joined, o)
        a2[o, :, 0:640] = s
        a2[o, :, 640:WIN] = t
    for o, target in zip(others_x, to_x):
        send(a2.at[o], a2_in.at[x], a2_recv.at[x], target)
    for o in others_x:
        receive(b1_in.at[o], b1_recv.at[o])
    joined = b1[x].astype(F32)
    for o in others_x:
        joined = joined + b1_in[o].astype(F32)
    joined = joined.astype(BF16)
    for o in range(NY):
        b2[o] = joined[o * 16 : (o + 1) * 16, :]
    for o, target in zip(others_y, to_y):
        send(b2.at[o], b2_in.at[y], b2_recv.at[y], target)

    for o in others_x:
        receive(a2_in.at[o], a2_recv.at[o])
    half_a = a2[x].astype(F32)
    for o in others_x:
        half_a = half_a + a2_in[o].astype(F32)
    for o in others_y:
        receive(b2_in.at[o], b2_recv.at[o])
    half_b = b2[y].astype(F32)
    for o in others_y:
        half_b = half_b + b2_in[o].astype(F32)
    for h, part in enumerate((half_a, half_b)):
        for q in range(4):
            four = part[q * 4 : (q + 1) * 4, :]
            for hi in range(NZH):
                z1[hi * 8 + h * 4 + q, :, 0:384] = four[:, hi * 256 : hi * 256 + 384].astype(BF16)
                z1[hi * 8 + h * 4 + q, :, 384:ZWIN] = four[:, 640:WIN].astype(BF16)
    for o, target in zip(others_z, to_z):
        send(z1.at[o], z_in.at[at_z], zs_recv.at[at_z], target)

    gathered(line_b, line_b_recv, in_line)
    sums_b = total(line_b, 8)
    pair_b[zh] = sums_b
    send(pair_b.at[zh], pair_b.at[zh], pair_b_recv.at[zh], to_far)
    means = group_totals(sums_b * gains) / (FRAMES_CELLS * (C // GROUPS))
    inner = (grad_white - means[1:2] - whitened * means[0:1]) * inv
    grad_latents[...] = (cot[...].astype(F32) + inner).astype(BF16)
    store(grad_latents, latents_hbm)
    receive(pair_b.at[1 - zh], pair_b_recv.at[1 - zh])
    row_b[x] = pair_b[0] + pair_b[1]
    for target in to_x:
        send(row_b.at[x], row_b.at[x], row_b_recv.at[x], target)

    scale = 1.0 / math.sqrt(131072)
    for o in others_z:
        receive(z_in.at[o], zs_recv.at[o])
    result = z1[at_z].astype(F32)
    for o in others_z:
        result = result + z_in[o].astype(F32)
    grad_sums[...] = result * scale
    store(grad_sums, sums_hbm)
    for o in others_x:
        receive(row_b.at[o], row_b_recv.at[o])
    grad_norm[...] = total(row_b, 4) * scale
    store(grad_norm, norm_hbm)
    for copy in stores:
        copy.wait()
    for copy in pending:
        copy.wait_send()


def main(lat, cot, ws, wt, gain, bias):
    hbm = pl.BlockSpec(memory_space=pltpu.HBM)
    dma = pltpu.SemaphoreType.DMA
    V = pltpu.VMEM
    return pl.pallas_call(
        main_kernel,
        name="main",
        out_shape=(
            jax.ShapeDtypeStruct((ROWS, C), BF16),
            jax.ShapeDtypeStruct((ROWS, C), BF16),
            jax.ShapeDtypeStruct((4, ZWIN), F32),
            jax.ShapeDtypeStruct((2, C), F32),
        ),
        in_specs=[hbm] * 6,
        out_specs=(hbm,) * 4,
        scratch_shapes=[
            V((ROWS, C), BF16), V((ROWS, C), BF16), V((4, ZWIN), F32), V((2, C), F32),
            V((ROWS, C), BF16), V((ROWS, C), BF16), V((1, C), F32), V((1, C), F32),
            V((ROWS, C), BF16), V((ROWS, C), BF16), V((NZH, NX, 384, C), BF16),
            V((8, 2, C), F32), V((8, 2, C), F32), V((8, 2, C), F32), V((8, 2, C), F32),
            V((NZH, 2, C), F32), V((NX, 2, C), F32),
            V((9 * C, C), BF16), V((3 * C, C), BF16),
            V((2 * ROWS, 9 * C), BF16), V((2 * ROWS, C), BF16), V((ROWS, 3 * C), BF16),
            V((ROWS, 9 * C), BF16), V((C, ROWS), BF16), V((C, ROWS), BF16),
            V((128, 12 * C), BF16), V((128, 12 * C), F32), V((128, 12 * C), BF16),
            V((NY, 16, 12 * C), BF16), V((NX, 64, WIN), BF16),
            V((NY, 16, 12 * C), BF16), V((NX, 64, WIN), BF16),
            V((NX, 16, WIN), BF16), V((NY, 16, WIN), BF16),
            V((NX, 16, WIN), BF16), V((NY, 16, WIN), BF16),
            V((16, 4, ZWIN), BF16), V((16, 4, ZWIN), BF16),
            dma((6,)), dma((4,)), dma((SENDS,)),
            dma((8,)), dma((8,)), dma((8,)), dma((8,)), dma((2,)), dma((4,)),
            dma((2,)), dma((4,)), dma((1,)), dma((4,)), dma((4,)), dma((4,)), dma((1,)),
            dma((2,)), dma((4,)), dma((4,)), dma((4,)), dma((4,)), dma((16,)),
        ],
        compiler_params=pltpu.CompilerParams(
            collective_id=1, has_side_effects=True, vmem_limit_bytes=VMEM_BYTES
        ),
    )(lat, cot, ws, wt, gain, bias)


def finish_kernel(
    main_out, main_latents, main_sums, main_norms,
    out_hbm, latents_hbm, spatial_hbm, temporal_hbm, norm_hbm,
    sums, norms, block_out, grad_latents, spatial, temporal, norm, load_sem, store_sem,
):
    dp, wide = lax.axis_index("dp"), lax.axis_index("wide")
    copies = [
        pltpu.make_async_copy(main_sums, sums, load_sem.at[0]),
        pltpu.make_async_copy(main_norms, norms, load_sem.at[1]),
        pltpu.make_async_copy(main_out, block_out, load_sem.at[2]),
        pltpu.make_async_copy(main_latents, grad_latents, load_sem.at[3]),
    ]
    for copy in copies:
        copy.start()
    copies[0].wait()
    odd, hi = lax.rem(lax.div(dp, 2), 2), lax.rem(dp, 2)
    pick_s, pick_t = jnp.zeros((4, 288), F32), jnp.zeros((4, 96), F32)
    for at_odd in range(2):
        for at_hi in range(2):
            here = jnp.logical_and(odd == at_odd, hi == at_hi)
            s, t = 64 * at_odd + 32 * at_hi, 384 + 64 * at_odd + 96 * at_hi
            pick_s = jnp.where(here, sums[:, s : s + 288], pick_s)
            pick_t = jnp.where(here, sums[:, t : t + 96], pick_t)
    spatial[...] = pick_s
    temporal[...] = pick_t
    copies[1].wait()
    lane = lax.broadcasted_iota(jnp.int32, (2, C), 1)
    for k in range(4):
        norm[:, k : k + 1] = jnp.sum(
            jnp.where(lane == 4 * wide + k, norms[...], 0.0), axis=1, keepdims=True
        )
    copies[2].wait()
    copies[3].wait()
    stores = [
        pltpu.make_async_copy(source, target, store_sem.at[k])
        for k, (source, target) in enumerate(
            (
                (block_out, out_hbm),
                (grad_latents, latents_hbm),
                (spatial, spatial_hbm),
                (temporal, temporal_hbm),
                (norm, norm_hbm),
            )
        )
    ]
    for copy in stores:
        copy.start()
    for copy in stores:
        copy.wait()


def finish(*parts):
    hbm = pl.BlockSpec(memory_space=pltpu.HBM)
    dma = pltpu.SemaphoreType.DMA
    outs = [((ROWS, C), BF16), ((ROWS, C), BF16), ((4, 288), F32), ((4, 96), F32), ((2, 4), F32)]
    return pl.pallas_call(
        finish_kernel,
        name="finish",
        out_shape=[jax.ShapeDtypeStruct(*shape) for shape in outs],
        in_specs=[hbm] * 4,
        out_specs=[hbm] * 5,
        scratch_shapes=[pltpu.VMEM((4, ZWIN), F32), pltpu.VMEM((2, C), F32)]
        + [pltpu.VMEM(*shape) for shape in outs]
        + [dma((4,)), dma((5,))],
        compiler_params=pltpu.CompilerParams(vmem_limit_bytes=VMEM_BYTES),
    )(*parts)


def local(latents, cotangent, norm_gain, norm_bias, w_spatial, w_temporal):
    block_out, grad_latents, spatial, temporal, norm = finish(
        *main(
            latents.reshape(ROWS, C),
            cotangent.reshape(ROWS, C),
            w_spatial,
            w_temporal,
            norm_gain.reshape(1, C),
            norm_bias.reshape(1, C),
        )
    )
    return (
        block_out.reshape(latents.shape),
        grad_latents.reshape(latents.shape),
        spatial.T,
        temporal.T,
        norm,
    )


def solution(mesh):
    return jax.shard_map(
        local,
        mesh=mesh,
        in_specs=(
            P("dp", "wide", None, None, None),
            P("dp", "wide", None, None, None),
            P(),
            P(),
            P("dp", None),
            P("dp", None),
        ),
        out_specs=(
            P("dp", "wide", None, None, None),
            P("dp", "wide", None, None, None),
            P("dp", "wide"),
            P("dp", "wide"),
            P(None, "wide"),
        ),
        check_vma=False,
    )
```

```python
import math

import jax
import jax.numpy as jnp
from jax import lax
from jax.experimental import pallas as pl
from jax.experimental.pallas import tpu as pltpu
from jax.sharding import PartitionSpec as P

MESH = pl.DeviceIdType.MESH
F32 = jnp.float32
BF16 = jnp.bfloat16
GROUPS = 32
EPSILON = 1e-05
C = 256
CELLS = 128
COLS = 16
ROWS = 256
NX, NZH, NY, NZL, NC = 4, 2, 4, 8, 2
S_TILE = (0, 4, 9, 13)
T_TILE = (0, 1, 3, 4)
S_WIN = 5 * 128
T_WIN = 2 * 128
HALF = 128


def coords():
    dp, wide = lax.axis_index("dp"), lax.axis_index("wide")
    return (
        lax.div(dp, 2),
        lax.rem(dp, 2),
        lax.div(wide, 16),
        lax.rem(lax.div(wide, 2), 8),
        lax.rem(wide, 2),
    )


def device(x, zh, y, zl, c):
    return (x * 2 + zh, (y * 8 + zl) * 2 + c)


def remote(src, dst, send_sem, recv_sem, target):
    return pltpu.make_async_remote_copy(
        src_ref=src,
        dst_ref=dst,
        send_sem=send_sem,
        recv_sem=recv_sem,
        device_id=target,
        device_id_type=MESH,
    )


def greet(targets):
    barrier = pltpu.get_barrier_semaphore()
    for target in targets:
        pl.semaphore_signal(barrier, inc=1, device_id=target, device_id_type=MESH)
    return lambda: pl.semaphore_wait(barrier, len(targets))


def plane_peers(x, zh, y, zl, c):
    mine = y * 2 + c
    peers = []
    for k in range(1, 8):
        other = lax.rem(mine + k, 8)
        peers.append((other, device(x, zh, lax.div(other, 2), zl, lax.rem(other, 2))))
    return mine, peers


def line_peers(x, zh, y, zl, c):
    peers = []
    for k in range(1, 8):
        other = lax.rem(zl + k, 8)
        peers.append((other, device(x, zh, y, other, c)))
    return zl, peers


def total(slots, count):
    result = slots[0]
    for k in range(1, count):
        result = result + slots[k]
    return result


def group_ones():
    row = lax.broadcasted_iota(jnp.int32, (C, C), 0)
    col = lax.broadcasted_iota(jnp.int32, (C, C), 1)
    return (lax.div(row, C // GROUPS) == lax.div(col, C // GROUPS)).astype(F32)


def group_totals(two_rows):
    padded = jnp.concatenate([two_rows, jnp.zeros((6, C), F32)], axis=0)
    return jnp.dot(
        padded, group_ones(), precision=lax.Precision.HIGHEST, preferred_element_type=F32
    )


def column_iota(rows):
    return lax.rem(lax.broadcasted_iota(jnp.int32, (rows, C), 0), COLS)


def shifted(values, step):
    rows = values.shape[0]
    if step == 0:
        return values.astype(BF16)
    col = column_iota(rows)
    moved = pltpu.roll(values, (rows - step) % rows, 0)
    edge = COLS - 1 if step == 1 else 0
    return jnp.where(col == edge, 0.0, moved).astype(BF16)


def fill_windows(target, values, sign):
    frames = values.shape[0] // CELLS
    for dx in range(3):
        cols = shifted(values, sign * (dx - 1))
        for dy in range(3):
            step = sign * (dy - 1)
            lanes = pl.ds((3 * dy + dx) * C, C)
            if step == 0:
                target[:, lanes] = cols
                continue
            for frame in range(frames):
                base = frame * CELLS
                if step == 1:
                    target[base : base + CELLS - COLS, lanes] = cols[base + COLS : base + CELLS]
                    target[base + CELLS - COLS : base + CELLS, lanes] = jnp.zeros((COLS, C), BF16)
                else:
                    target[base + COLS : base + CELLS, lanes] = cols[base : base + CELLS - COLS]
                    target[base : base + COLS, lanes] = jnp.zeros((COLS, C), BF16)


def permutation(c):
    row = lax.broadcasted_iota(jnp.int32, (HALF, C), 0)
    col = lax.broadcasted_iota(jnp.int32, (HALF, C), 1)
    y, zl, j = lax.div(row, 32), lax.rem(lax.div(row, 4), 8), lax.rem(row, 4)
    return (col == y * 64 + zl * 8 + c * 4 + j).astype(F32).astype(BF16)


def times_transpose(left, right):
    return lax.dot_general(left, right, (((1,), (1,)), ((), ())), preferred_element_type=F32)


FRAMES_CELLS = 128 * CELLS


SENDS = 160
VMEM_BYTES = 62 << 20


def main_kernel(
    lat_hbm, cot_hbm, ws_hbm, wt_hbm, gain_hbm, bias_hbm,
    out_hbm, latents_hbm, s_hbm, t_hbm, norm_hbm,
    block_out, grad_latents, s_out, t_out, norm_out,
    frames, gain, bias, wsp, wtm,
    plane, line, plane_b, line_b, row_b, deep_b,
    w_sp, w_tm, windows, spatial, mixed, grad_act, adjoint, cot_t,
    s1, s1_in, t1, t1_in, zs, zs_in, zt, zt_in,
    local_sem, store_sem, send_sem,
    plane_recv, line_recv, plane_b_recv, line_b_recv, row_b_recv, deep_b_recv,
    mate_recv, halo_recv, pass_recv, tx_recv, tz_recv, txy_recv,
    sx_recv, sz_recv, sxy_recv, c1_recv, c2_recv, s1_recv, t1_recv, zs_recv, zt_recv,
):
    x, zh, y, zl, c = coords()
    wide, dp = lax.axis_index("wide"), lax.axis_index("dp")
    lat_at, cot_at, edge_out, edge_in = 1 + c, 3 + c, 3 - c, 5 - 5 * c
    lat, cot = frames.at[lat_at], frames.at[cot_at]
    loads = [
        pltpu.make_async_copy(source, target, local_sem.at[k])
        for k, (source, target) in enumerate(
            (
                (lat_hbm, lat),
                (wt_hbm, wtm.at[zh, x]),
                (ws_hbm, wsp.at[zh, x]),
                (cot_hbm, cot),
                (gain_hbm, gain),
                (bias_hbm, bias),
            )
        )
    ]
    for copy in loads:
        copy.start()
    mine, in_plane = plane_peers(x, zh, y, zl, c)
    _, in_line = line_peers(x, zh, y, zl, c)
    others_x = [lax.rem(x + k, NX) for k in (1, 2, 3)]
    to_x = [device(o, zh, y, zl, c) for o in others_x]
    to_c = device(x, zh, y, zl, 1 - c)
    to_far = device(x, 1 - zh, y, lax.rem(zl + 4, 8), c)
    ahead, behind = (dp, lax.rem(wide + 2, 64)), (dp, lax.rem(wide + 62, 64))
    edge_to = (dp, lax.rem(wide + 62 + 4 * c, 64))
    at_xy = x * 4 + y
    in_xy = []
    for k in range(1, 16):
        ox, oy = lax.rem(x + k // 4, NX), lax.rem(y + k % 4, NY)
        in_xy.append((ox * 4 + oy, device(ox, zh, oy, zl, c), ox, oy))
    at_z = zh * 8 + zl
    in_z = []
    for k in range(1, 16):
        o = lax.rem(at_z + k, 16)
        in_z.append((o, device(x, lax.div(o, 8), y, lax.rem(o, 8), c)))
    arrived = greet(
        [p for _, p in in_plane]
        + [p for _, p in in_line]
        + [in_xy[k - 1][1] for k in range(4, 16)]
        + [to_far, ahead, behind]
    )

    stores = []

    def store(source, target):
        copy = pltpu.make_async_copy(source, target, store_sem.at[len(stores)])
        copy.start()
        stores.append(copy)

    pending = []

    def send(ref, target, recv, where):
        copy = remote(ref, target, send_sem.at[len(pending)], recv, where)
        copy.start()
        pending.append(copy)

    def receive(ref, recv):
        remote(ref, ref, send_sem.at[0], recv, to_c).wait_recv()

    def exchange(slots, recv, at, peers):
        for _, target in peers:
            send(slots.at[at], slots.at[at], recv.at[at], target)

    def gathered(slots, recv, peers):
        for other, _ in peers:
            receive(slots.at[other], recv.at[other])

    loads[0].wait()
    wide_lat = lat[...].astype(F32)
    plane[mine, 0:1, :] = jnp.sum(wide_lat, axis=0, keepdims=True)
    plane[mine, 1:2, :] = jnp.sum(wide_lat * wide_lat, axis=0, keepdims=True)
    for copy in loads[1:]:
        copy.wait()
    arrived()

    exchange(plane, plane_recv, mine, in_plane)
    lanes = pl.ds(pl.multiple_of(c * HALF, HALF), HALF)
    t_rows = pl.ds(y * 3, 3)
    s_rows = pl.ds(y * 9, 9)
    part = wtm.at[zh, x, t_rows]
    send(part, part, tz_recv.at[0], to_far)
    part = wsp.at[zh, x, s_rows, :, lanes]
    send(part, part, sz_recv.at[0], to_far)
    for target in to_x:
        send(wtm.at[zh, x], wtm.at[zh, x], tx_recv.at[x], target)
    send(lat, lat, mate_recv.at[0], to_c)
    send(cot, cot, mate_recv.at[1], to_c)
    send(frames.at[edge_out], frames.at[edge_in], halo_recv.at[0], edge_to)
    part = wsp.at[zh, x, :, :, lanes]
    for target in to_x:
        send(part, part, sx_recv.at[x], target)

    gathered(plane, plane_recv, in_plane)
    line[zl] = total(plane, 8)
    exchange(line, line_recv, zl, in_line)

    part = wtm.at[1 - zh, x, t_rows]
    receive(part, tz_recv.at[0])
    for _, target, _, _ in in_xy:
        send(part, part, txy_recv.at[at_xy], target)
    part = wsp.at[1 - zh, x, s_rows, :, lanes]
    receive(part, sz_recv.at[0])
    for _, target, _, _ in in_xy:
        send(part, part, sxy_recv.at[at_xy], target)
    receive(frames.at[edge_in], halo_recv.at[0])
    send(frames.at[edge_in], frames.at[edge_in], pass_recv.at[0], to_c)
    for o in others_x:
        part = wsp.at[zh, o, :, :, lanes]
        receive(part, sx_recv.at[o])
        send(part, part, c1_recv.at[o], to_c)
    receive(frames.at[2 - c], mate_recv.at[0])
    receive(frames.at[4 - c], mate_recv.at[1])
    order = permutation(c)
    for k in range(2):
        cot_t[:, k * ROWS : (k + 1) * ROWS] = times_transpose(order, frames[3 + k]).astype(BF16)

    gathered(line, line_recv, in_line)
    sums = group_totals(total(line, 8)) / (FRAMES_CELLS * (C // GROUPS))
    mean = sums[0:1]
    inv = 1.0 / jnp.sqrt(sums[1:2] - mean * mean + EPSILON)
    gains, biases = gain[...], bias[...]

    def normed_of(values):
        whitened = (values.astype(F32) - mean) * inv
        return whitened, whitened * gains + biases

    for k in (1, 2):
        _, normed = normed_of(frames[k])
        fill_windows(
            windows.at[k * ROWS : (k + 1) * ROWS, :], normed * jax.nn.sigmoid(normed), 1
        )

    receive(frames.at[5 * c], pass_recv.at[0])
    last = frames[5]
    later = jnp.where(wide < 62, last.astype(F32), 0.0).astype(BF16)
    for o in others_x:
        receive(wtm.at[zh, o], tx_recv.at[o])
    for slot, _, ox, oy in in_xy:
        receive(wtm.at[1 - zh, ox, pl.ds(oy * 3, 3)], txy_recv.at[slot])
    for d in range(8):
        w_tm[d * 96 : (d + 1) * 96, :] = wtm[d % 2, d // 2].reshape(96, C)
    held = jnp.concatenate([frames[3], frames[4], later], axis=0)
    running = jnp.zeros((2 * ROWS, C), F32)
    for delay in range(3):
        start = delay * CELLS
        running = running + times_transpose(
            held[start : start + 2 * ROWS], w_tm[delay * C : (delay + 1) * C, :]
        )
    grad_act[...] = running.astype(BF16)
    act_t = times_transpose(order, grad_act[...]).astype(BF16)
    for o in range(NX):
        start = S_TILE[o] * 128
        piece = jnp.dot(
            act_t, windows[ROWS:, start : start + S_WIN], preferred_element_type=F32
        ).astype(BF16)
        for p in range(NY):
            s1[o * 4 + p] = piece[p * 32 : (p + 1) * 32, :]
    for slot, target, _, _ in in_xy:
        send(s1.at[slot], s1_in.at[at_xy], s1_recv.at[at_xy], target)

    own_rows = pl.ds(pl.multiple_of(c * ROWS, ROWS), ROWS)
    fill_windows(adjoint, grad_act[own_rows, :].astype(F32), -1)
    _, normed = normed_of(frames[0])
    fill_windows(windows.at[0:ROWS, :], normed * jax.nn.sigmoid(normed), 1)

    for slot, _, ox, oy in in_xy:
        receive(wsp.at[1 - zh, ox, pl.ds(oy * 9, 9), :, lanes], sxy_recv.at[slot])
    part = wsp.at[1 - zh, :, :, :, lanes]
    send(part, part, c2_recv.at[0], to_c)
    other_lanes = pl.ds(pl.multiple_of((1 - c) * HALF, HALF), HALF)
    for o in others_x:
        receive(wsp.at[zh, o, :, :, other_lanes], c1_recv.at[o])
    receive(wsp.at[1 - zh, :, :, :, other_lanes], c2_recv.at[0])
    for d in range(8):
        w_sp[d * 288 : (d + 1) * 288, :] = wsp[d % 2, d // 2].reshape(288, C)

    running = jnp.zeros((ROWS, C), F32)
    for tap in range(9):
        taps = slice(tap * C, (tap + 1) * C)
        running = running + times_transpose(adjoint[:, taps], w_sp[taps, :])
    whitened, normed = normed_of(lat[...])
    sigmoid = jax.nn.sigmoid(normed)
    grad_normed = running * (sigmoid * (1.0 + normed * (1.0 - sigmoid)))
    plane_b[mine, 0:1, :] = jnp.sum(grad_normed * whitened, axis=0, keepdims=True)
    plane_b[mine, 1:2, :] = jnp.sum(grad_normed, axis=0, keepdims=True)
    exchange(plane_b, plane_b_recv, mine, in_plane)
    grad_white = grad_normed * gains

    conv = jnp.dot(windows[...], w_sp[...], preferred_element_type=F32)
    spatial[ROWS:, :] = conv[ROWS:].astype(BF16)
    spatial[:ROWS, :] = jnp.where(wide > 1, conv[:ROWS], 0.0).astype(BF16)
    for delay in range(3):
        start = (2 - delay) * CELLS
        mixed[:, delay * C : (delay + 1) * C] = spatial[start : start + 2 * ROWS, :]
    for o in range(NX):
        start = T_TILE[o] * 128
        piece = jnp.dot(
            cot_t[...], mixed[:, start : start + T_WIN], preferred_element_type=F32
        ).astype(BF16)
        for p in range(NY):
            t1[o * 4 + p] = piece[p * 32 : (p + 1) * 32, :]
    for slot, target, _, _ in in_xy:
        send(t1.at[slot], t1_in.at[at_xy], t1_recv.at[at_xy], target)
    temporal = jnp.dot(mixed[own_rows, :], w_tm[...], preferred_element_type=F32)
    block_out[...] = (lat[...].astype(F32) + temporal).astype(BF16)
    store(block_out, out_hbm)

    gathered(plane_b, plane_b_recv, in_plane)
    sums_b = total(plane_b, 8)
    line_b[zl] = sums_b
    row_b[x] = sums_b
    exchange(line_b, line_b_recv, zl, in_line)
    for target in to_x:
        send(row_b.at[x], row_b.at[x], row_b_recv.at[x], target)

    odd = lax.rem(x, 2)

    def across_z(slots, slots_in, recv, source, source_in, source_recv, width):
        for slot, _, _, _ in in_xy:
            receive(source_in.at[slot], source_recv.at[slot])
        joined = source[at_xy].astype(F32)
        for slot, _, _, _ in in_xy:
            joined = joined + source_in[slot].astype(F32)
        for hi in range(NZH):
            at = width * hi
            mid = jnp.where(
                odd == 1, joined[:, at + 64 : at + 64 + width], joined[:, at : at + width]
            )
            for q in range(8):
                slots[hi * 8 + q, :, 0:width] = mid[q * 4 : (q + 1) * 4].astype(BF16)
                slots[hi * 8 + q, :, width:] = jnp.zeros((4, slots.shape[2] - width), BF16)
        for o, target in in_z:
            send(slots.at[o], slots_in.at[at_z], recv.at[at_z], target)

    scale = 1.0 / math.sqrt(131072)

    def at_last(slots, slots_in, recv, out, out_hbm):
        for o, _ in in_z:
            receive(slots_in.at[o], recv.at[o])
        result = slots[at_z].astype(F32)
        for o, _ in in_z:
            result = result + slots_in[o].astype(F32)
        out[...] = result * scale
        store(out, out_hbm)

    across_z(zs, zs_in, zs_recv, s1, s1_in, s1_recv, 288)
    for o in others_x:
        receive(row_b.at[o], row_b_recv.at[o])
    deep_b[at_z] = total(row_b, 4)
    for _, target in in_z:
        send(deep_b.at[at_z], deep_b.at[at_z], deep_b_recv.at[at_z], target)
    across_z(zt, zt_in, zt_recv, t1, t1_in, t1_recv, 96)

    gathered(line_b, line_b_recv, in_line)
    means = group_totals(total(line_b, 8) * gains) / (FRAMES_CELLS * (C // GROUPS))
    inner = (grad_white - means[1:2] - whitened * means[0:1]) * inv
    grad_latents[...] = (cot[...].astype(F32) + inner).astype(BF16)
    store(grad_latents, latents_hbm)

    at_last(zs, zs_in, zs_recv, s_out, s_hbm)
    for o, _ in in_z:
        receive(deep_b.at[o], deep_b_recv.at[o])
    norm_out[...] = total(deep_b, 16) * scale
    store(norm_out, norm_hbm)
    at_last(zt, zt_in, zt_recv, t_out, t_hbm)
    for copy in stores:
        copy.wait()
    for copy in pending:
        copy.wait_send()


MAIN_OUTS = (
    ((ROWS, C), BF16), ((ROWS, C), BF16), ((4, 384), F32), ((4, 128), F32), ((2, C), F32),
)


def main(lat, cot, ws, wt, gain, bias):
    hbm = pl.BlockSpec(memory_space=pltpu.HBM)
    dma = pltpu.SemaphoreType.DMA
    V = pltpu.VMEM
    return pl.pallas_call(
        main_kernel,
        name="main",
        out_shape=[jax.ShapeDtypeStruct(*shape) for shape in MAIN_OUTS],
        in_specs=[hbm] * 6,
        out_specs=[hbm] * 5,
        scratch_shapes=[V(*shape) for shape in MAIN_OUTS]
        + [
            V((6, ROWS, C), BF16), V((1, C), F32), V((1, C), F32),
            V((NZH, NX, 36, 8, C), BF16), V((NZH, NX, 12, 8, C), BF16),
            V((8, 2, C), F32), V((8, 2, C), F32), V((8, 2, C), F32), V((8, 2, C), F32),
            V((NX, 2, C), F32), V((16, 2, C), F32),
            V((9 * C, C), BF16), V((3 * C, C), BF16),
            V((3 * ROWS, 9 * C), BF16), V((3 * ROWS, C), BF16), V((2 * ROWS, 3 * C), BF16),
            V((2 * ROWS, C), BF16), V((ROWS, 9 * C), BF16), V((HALF, 2 * ROWS), BF16),
            V((16, 32, S_WIN), BF16), V((16, 32, S_WIN), BF16),
            V((16, 32, T_WIN), BF16), V((16, 32, T_WIN), BF16),
            V((16, 4, 384), BF16), V((16, 4, 384), BF16),
            V((16, 4, 128), BF16), V((16, 4, 128), BF16),
            dma((6,)), dma((5,)), dma((SENDS,)),
            dma((8,)), dma((8,)), dma((8,)), dma((8,)), dma((4,)), dma((16,)),
            dma((2,)), dma((1,)), dma((1,)), dma((4,)), dma((1,)), dma((16,)),
            dma((4,)), dma((1,)), dma((16,)), dma((4,)), dma((1,)),
            dma((16,)), dma((16,)), dma((16,)), dma((16,)),
        ],
        compiler_params=pltpu.CompilerParams(
            collective_id=1, has_side_effects=True, vmem_limit_bytes=VMEM_BYTES
        ),
    )(lat, cot, ws, wt, gain, bias)


def finish_kernel(
    main_out, main_latents, main_s, main_t, main_norms,
    out_hbm, latents_hbm, spatial_hbm, temporal_hbm, norm_hbm,
    block_out, grad_latents, sums_s, sums_t, norms, spatial, temporal, norm,
    load_sem, store_sem,
):
    wide = lax.axis_index("wide")
    loads = [
        pltpu.make_async_copy(source, target, load_sem.at[k])
        for k, (source, target) in enumerate(
            (
                (main_norms, norms),
                (main_s, sums_s),
                (main_t, sums_t),
                (main_out, block_out),
                (main_latents, grad_latents),
            )
        )
    ]
    for copy in loads:
        copy.start()
    loads[0].wait()
    lane = lax.broadcasted_iota(jnp.int32, (2, C), 1)
    for k in range(4):
        norm[:, k : k + 1] = jnp.sum(
            jnp.where(lane == 4 * wide + k, norms[...], 0.0), axis=1, keepdims=True
        )
    loads[1].wait()
    spatial[...] = sums_s[:, :288]
    loads[2].wait()
    temporal[...] = sums_t[:, :96]
    loads[3].wait()
    loads[4].wait()
    stores = [
        pltpu.make_async_copy(source, target, store_sem.at[k])
        for k, (source, target) in enumerate(
            (
                (block_out, out_hbm),
                (grad_latents, latents_hbm),
                (spatial, spatial_hbm),
                (temporal, temporal_hbm),
                (norm, norm_hbm),
            )
        )
    ]
    for copy in stores:
        copy.start()
    for copy in stores:
        copy.wait()


def finish(*parts):
    hbm = pl.BlockSpec(memory_space=pltpu.HBM)
    dma = pltpu.SemaphoreType.DMA
    last = [((4, 288), F32), ((4, 96), F32), ((2, 4), F32)]
    return pl.pallas_call(
        finish_kernel,
        name="finish",
        out_shape=[jax.ShapeDtypeStruct(*shape) for shape in list(MAIN_OUTS[:2]) + last],
        in_specs=[hbm] * 5,
        out_specs=[hbm] * 5,
        scratch_shapes=[pltpu.VMEM(*shape) for shape in list(MAIN_OUTS) + last]
        + [dma((5,)), dma((5,))],
        compiler_params=pltpu.CompilerParams(vmem_limit_bytes=VMEM_BYTES),
    )(*parts)


def local(latents, cotangent, norm_gain, norm_bias, w_spatial, w_temporal):
    block_out, grad_latents, spatial, temporal, norm = finish(
        *main(
            latents.reshape(ROWS, C),
            cotangent.reshape(ROWS, C),
            w_spatial.reshape(36, 8, C),
            w_temporal.reshape(12, 8, C),
            norm_gain.reshape(1, C),
            norm_bias.reshape(1, C),
        )
    )
    return (
        block_out.reshape(latents.shape),
        grad_latents.reshape(latents.shape),
        spatial.T,
        temporal.T,
        norm,
    )


def solution(mesh):
    return jax.shard_map(
        local,
        mesh=mesh,
        in_specs=(
            P("dp", "wide", None, None, None),
            P("dp", "wide", None, None, None),
            P(),
            P(),
            P("dp", None),
            P("dp", None),
        ),
        out_specs=(
            P("dp", "wide", None, None, None),
            P("dp", "wide", None, None, None),
            P("dp", "wide"),
            P("dp", "wide"),
            P(None, "wide"),
        ),
        check_vma=False,
    )
```

```python
import math

import jax
import jax.numpy as jnp
from jax import lax
from jax.experimental import pallas as pl
from jax.experimental.pallas import tpu as pltpu
from jax.sharding import PartitionSpec as P

MESH = pl.DeviceIdType.MESH
F32 = jnp.float32
BF16 = jnp.bfloat16
GROUPS = 32
EPSILON = 1e-05
C = 256
CELLS = 128
COLS = 16
ROWS = 256
NX, NZH, NY, NZL, NC = 4, 2, 4, 8, 2
S_WIN = 5 * 128
T_WIN = 2 * 128
HALF = 128


def coords():
    dp, wide = lax.axis_index("dp"), lax.axis_index("wide")
    return (
        lax.div(dp, 2),
        lax.rem(dp, 2),
        lax.div(wide, 16),
        lax.rem(lax.div(wide, 2), 8),
        lax.rem(wide, 2),
    )


def device(x, zh, y, zl, c):
    return (x * 2 + zh, (y * 8 + zl) * 2 + c)


def remote(src, dst, send_sem, recv_sem, target):
    return pltpu.make_async_remote_copy(
        src_ref=src,
        dst_ref=dst,
        send_sem=send_sem,
        recv_sem=recv_sem,
        device_id=target,
        device_id_type=MESH,
    )


def greet(targets):
    barrier = pltpu.get_barrier_semaphore()
    for target in targets:
        pl.semaphore_signal(barrier, inc=1, device_id=target, device_id_type=MESH)
    return lambda: pl.semaphore_wait(barrier, len(targets))


def plane_peers(x, zh, y, zl, c):
    mine = y * 2 + c
    peers = []
    for k in range(1, 8):
        other = lax.rem(mine + k, 8)
        peers.append((other, device(x, zh, lax.div(other, 2), zl, lax.rem(other, 2))))
    return mine, peers


def line_peers(x, zh, y, zl, c):
    peers = []
    for k in range(1, 8):
        other = lax.rem(zl + k, 8)
        peers.append((other, device(x, zh, y, other, c)))
    return zl, peers


def total(slots, count):
    result = slots[0]
    for k in range(1, count):
        result = result + slots[k]
    return result


def group_ones():
    row = lax.broadcasted_iota(jnp.int32, (C, C), 0)
    col = lax.broadcasted_iota(jnp.int32, (C, C), 1)
    return (lax.div(row, C // GROUPS) == lax.div(col, C // GROUPS)).astype(F32)


def group_totals(two_rows):
    padded = jnp.concatenate([two_rows, jnp.zeros((6, C), F32)], axis=0)
    return jnp.dot(
        padded, group_ones(), precision=lax.Precision.HIGHEST, preferred_element_type=F32
    )


def column_iota(rows):
    return lax.rem(lax.broadcasted_iota(jnp.int32, (rows, C), 0), COLS)


def shifted(values, step):
    rows = values.shape[0]
    if step == 0:
        return values.astype(BF16)
    col = column_iota(rows)
    moved = pltpu.roll(values, (rows - step) % rows, 0)
    edge = COLS - 1 if step == 1 else 0
    return jnp.where(col == edge, 0.0, moved).astype(BF16)


def fill_windows(target, values, sign):
    frames = values.shape[0] // CELLS
    for dx in range(3):
        cols = shifted(values, sign * (dx - 1))
        for dy in range(3):
            step = sign * (dy - 1)
            lanes = pl.ds((3 * dy + dx) * C, C)
            if step == 0:
                target[:, lanes] = cols
                continue
            for frame in range(frames):
                base = frame * CELLS
                if step == 1:
                    target[base : base + CELLS - COLS, lanes] = cols[base + COLS : base + CELLS]
                    target[base + CELLS - COLS : base + CELLS, lanes] = jnp.zeros((COLS, C), BF16)
                else:
                    target[base + COLS : base + CELLS, lanes] = cols[base : base + CELLS - COLS]
                    target[base : base + COLS, lanes] = jnp.zeros((COLS, C), BF16)


def permutation(c):
    row = lax.broadcasted_iota(jnp.int32, (HALF, C), 0)
    col = lax.broadcasted_iota(jnp.int32, (HALF, C), 1)
    y, zl, j = lax.div(row, 32), lax.rem(lax.div(row, 4), 8), lax.rem(row, 4)
    return (col == y * 64 + zl * 8 + c * 4 + j).astype(F32).astype(BF16)


def times_transpose(left, right):
    return lax.dot_general(left, right, (((1,), (1,)), ((), ())), preferred_element_type=F32)


FRAMES_CELLS = 128 * CELLS


SENDS = 160
VMEM_BYTES = 40 << 20


def main_kernel(
    lat_hbm, cot_hbm, ws_hbm, wt_hbm, gain_hbm, bias_hbm,
    block_out, grad_latents, s_out, t_out, norm_out,
    frames, gain, bias, wsp, wtm,
    plane, line, plane_b, line_b, row_b, deep_b,
    windows, spatial, mixed, grad_act, adjoint, cot_t,
    s1, s1_in, t1, t1_in, zs, zs_in, zt, zt_in,
    local_sem, send_sem,
    plane_recv, line_recv, plane_b_recv, line_b_recv, row_b_recv, deep_b_recv,
    mate_recv, halo_recv, pass_recv, tx_recv, tz_recv, txy_recv,
    sx_recv, sz_recv, sxy_recv, c1_recv, c2_recv, s1_recv, t1_recv, zs_recv, zt_recv,
):
    x, zh, y, zl, c = coords()
    wide, dp = lax.axis_index("wide"), lax.axis_index("dp")
    lat_at, cot_at, edge_out, edge_in = 1 + c, 3 + c, 3 - c, 5 - 5 * c
    lat, cot = frames.at[lat_at], frames.at[cot_at]
    mine, in_plane = plane_peers(x, zh, y, zl, c)
    _, in_line = line_peers(x, zh, y, zl, c)
    others_x = [lax.rem(x + k, NX) for k in (1, 2, 3)]
    to_x = [device(o, zh, y, zl, c) for o in others_x]
    to_c = device(x, zh, y, zl, 1 - c)
    to_far = device(x, 1 - zh, y, lax.rem(zl + 4, 8), c)
    ahead, behind = (dp, lax.rem(wide + 2, 64)), (dp, lax.rem(wide + 62, 64))
    edge_to = (dp, lax.rem(wide + 62 + 4 * c, 64))
    at_xy = x * 4 + y
    in_xy = []
    for k in range(1, 16):
        ox, oy = lax.rem(x + k // 4, NX), lax.rem(y + k % 4, NY)
        in_xy.append((ox * 4 + oy, device(ox, zh, oy, zl, c), ox, oy))
    at_z = zh * 8 + zl
    in_z = []
    for k in range(1, 16):
        o = lax.rem(at_z + k, 16)
        in_z.append((o, device(x, lax.div(o, 8), y, lax.rem(o, 8), c)))
    arrived = greet(
        [p for _, p in in_line]
        + [to_far, ahead, behind]
        + [in_xy[k - 1][1] for k in range(4, 16)]
        + [p for _, p in in_plane]
    )

    loads = [
        pltpu.make_async_copy(source, target, local_sem.at[k])
        for k, (source, target) in enumerate(
            (
                (lat_hbm, lat),
                (wt_hbm, wtm.at[pl.ds(12 * dp, 12)]),
                (ws_hbm, wsp.at[pl.ds(36 * dp, 36)]),
                (cot_hbm, cot),
                (gain_hbm, gain),
                (bias_hbm, bias),
            )
        )
    ]
    for copy in loads:
        copy.start()

    pending = []

    def send(ref, target, recv, where):
        copy = remote(ref, target, send_sem.at[len(pending)], recv, where)
        copy.start()
        pending.append(copy)

    drained = [0]

    def drain():
        for copy in pending[drained[0] :]:
            copy.wait_send()
        drained[0] = len(pending)

    def receive(ref, recv):
        remote(ref, ref, send_sem.at[0], recv, to_c).wait_recv()

    def exchange(slots, recv, at, peers):
        for _, target in peers:
            send(slots.at[at], slots.at[at], recv.at[at], target)

    def gathered(slots, recv, peers):
        for other, _ in peers:
            receive(slots.at[other], recv.at[other])

    loads[0].wait()
    wide_lat = lat[...].astype(F32)
    plane[mine, 0:1, :] = jnp.sum(wide_lat, axis=0, keepdims=True)
    plane[mine, 1:2, :] = jnp.sum(wide_lat * wide_lat, axis=0, keepdims=True)
    for copy in loads[1:]:
        copy.wait()
    arrived()

    def t_shard(hi, at):
        return wtm.at[pl.ds(12 * (2 * at + hi), 12)]

    def t_piece(at, quarter):
        return wtm.at[pl.ds(12 * (2 * at + 1 - zh) + 3 * quarter, 3)]

    def s_shard(hi, at, lanes):
        return wsp.at[pl.ds(36 * (2 * at + hi), 36), :, lanes]

    def s_piece(at, quarter, lanes):
        return wsp.at[pl.ds(36 * (2 * at + 1 - zh) + 9 * quarter, 9), :, lanes]

    part = wtm.at[pl.ds(12 * dp + 3 * y, 3)]
    send(part, part, tz_recv.at[0], to_far)
    exchange(plane, plane_recv, mine, in_plane)
    lanes = pl.ds(pl.multiple_of(c * HALF, HALF), HALF)
    part = wsp.at[pl.ds(36 * dp + 9 * y, 9), :, lanes]
    send(part, part, sz_recv.at[0], to_far)
    for target in to_x:
        send(t_shard(zh, x), t_shard(zh, x), tx_recv.at[x], target)
    send(lat, lat, mate_recv.at[0], to_c)
    send(cot, cot, mate_recv.at[1], to_c)
    send(frames.at[edge_out], frames.at[edge_in], halo_recv.at[0], edge_to)
    part = s_shard(zh, x, lanes)
    for target in to_x:
        send(part, part, sx_recv.at[x], target)

    gathered(plane, plane_recv, in_plane)
    line[zl] = total(plane, 8)
    exchange(line, line_recv, zl, in_line)

    part = t_piece(x, y)
    receive(part, tz_recv.at[0])
    for _, target, _, _ in in_xy:
        send(part, part, txy_recv.at[at_xy], target)
    part = s_piece(x, y, lanes)
    receive(part, sz_recv.at[0])
    for _, target, _, _ in in_xy:
        send(part, part, sxy_recv.at[at_xy], target)
    receive(frames.at[edge_in], halo_recv.at[0])
    send(frames.at[edge_in], frames.at[edge_in], pass_recv.at[0], to_c)
    for o in others_x:
        part = s_shard(zh, o, lanes)
        receive(part, sx_recv.at[o])
        send(part, part, c1_recv.at[o], to_c)
    receive(frames.at[2 - c], mate_recv.at[0])
    receive(frames.at[4 - c], mate_recv.at[1])
    order = permutation(c)
    for k in range(2):
        cot_t[:, k * ROWS : (k + 1) * ROWS] = times_transpose(order, frames[3 + k]).astype(BF16)

    gathered(line, line_recv, in_line)
    sums = group_totals(total(line, 8)) / (FRAMES_CELLS * (C // GROUPS))
    mean = sums[0:1]
    inv = 1.0 / jnp.sqrt(sums[1:2] - mean * mean + EPSILON)
    gains, biases = gain[...], bias[...]

    def normed_of(values):
        whitened = (values.astype(F32) - mean) * inv
        return whitened, whitened * gains + biases

    for k in (1, 2):
        _, normed = normed_of(frames[k])
        fill_windows(
            windows.at[k * ROWS : (k + 1) * ROWS, :], normed * jax.nn.sigmoid(normed), 1
        )

    receive(frames.at[5 * c], pass_recv.at[0])
    last = frames[5]
    later = jnp.where(wide < 62, last.astype(F32), 0.0).astype(BF16)
    for o in others_x:
        receive(t_shard(zh, o), tx_recv.at[o])
    for slot, _, ox, oy in in_xy:
        receive(t_piece(ox, oy), txy_recv.at[slot])
    held = jnp.concatenate([frames[3], frames[4], later], axis=0)
    running = jnp.zeros((2 * ROWS, C), F32)
    for delay in range(3):
        start = delay * CELLS
        running = running + times_transpose(
            held[start : start + 2 * ROWS], wtm[delay * 32 : (delay + 1) * 32].reshape(C, C)
        )
    grad_act[...] = running.astype(BF16)
    act_t = times_transpose(order, grad_act[...]).astype(BF16)

    def scatter(left, right, slots, slots_in, recv, tiles, width, between):
        for k in (1, 2, 3, 0):
            o = lax.rem(x + k, NX)
            start = pl.multiple_of(lax.div(tiles * o, 2) * 128, 128)
            piece = jnp.dot(
                left, right(pl.ds(start, width)), preferred_element_type=F32
            ).astype(BF16)
            for p in range(NY):
                slots[o * 4 + p] = piece[p * 32 : (p + 1) * 32, :]
            for slot, target, ox, _ in in_xy[max(4 * k - 1, 0) : 4 * k + 3]:
                send(slots.at[slot], slots_in.at[at_xy], recv.at[at_xy], target)
            between(k, o)

    def pass_weights(k, o):
        for slot, _, ox, oy in in_xy[max(4 * k - 1, 0) : 4 * k + 3]:
            receive(s_piece(ox, oy, lanes), sxy_recv.at[slot])
        part = s_shard(1 - zh, o, lanes)
        send(part, part, c2_recv.at[o], to_c)

    scatter(act_t, lambda at: windows[ROWS:, at], s1, s1_in, s1_recv, 9, S_WIN, lambda k, o: None)

    own_rows = pl.ds(pl.multiple_of(c * ROWS, ROWS), ROWS)
    fill_windows(adjoint, grad_act[own_rows, :].astype(F32), -1)
    _, normed = normed_of(frames[0])
    fill_windows(windows.at[0:ROWS, :], normed * jax.nn.sigmoid(normed), 1)

    for k in (1, 2, 3, 0):
        pass_weights(k, lax.rem(x + k, NX))
    other_lanes = pl.ds(pl.multiple_of((1 - c) * HALF, HALF), HALF)
    for o in others_x:
        receive(s_shard(zh, o, other_lanes), c1_recv.at[o])
    for o in range(NX):
        receive(s_shard(1 - zh, o, other_lanes), c2_recv.at[o])

    running = jnp.zeros((ROWS, C), F32)
    for tap in range(9):
        taps = slice(tap * C, (tap + 1) * C)
        running = running + times_transpose(
            adjoint[:, taps], wsp[tap * 32 : (tap + 1) * 32].reshape(C, C)
        )
    whitened, normed = normed_of(lat[...])
    sigmoid = jax.nn.sigmoid(normed)
    grad_normed = running * (sigmoid * (1.0 + normed * (1.0 - sigmoid)))
    plane_b[mine, 0:1, :] = jnp.sum(grad_normed * whitened, axis=0, keepdims=True)
    plane_b[mine, 1:2, :] = jnp.sum(grad_normed, axis=0, keepdims=True)
    exchange(plane_b, plane_b_recv, mine, in_plane)
    grad_white = grad_normed * gains

    conv = jnp.dot(windows[...], wsp[...].reshape(9 * C, C), preferred_element_type=F32)
    spatial[ROWS:, :] = conv[ROWS:].astype(BF16)
    spatial[:ROWS, :] = jnp.where(wide > 1, conv[:ROWS], 0.0).astype(BF16)
    for delay in range(3):
        start = (2 - delay) * CELLS
        mixed[:, delay * C : (delay + 1) * C] = spatial[start : start + 2 * ROWS, :]
    scatter(cot_t[...], lambda at: mixed[:, at], t1, t1_in, t1_recv, 3, T_WIN, lambda k, o: None)
    temporal = jnp.dot(
        mixed[own_rows, :], wtm[...].reshape(3 * C, C), preferred_element_type=F32
    )
    block_out[...] = (lat[...].astype(F32) + temporal).astype(BF16)

    gathered(plane_b, plane_b_recv, in_plane)
    sums_b = total(plane_b, 8)
    line_b[zl] = sums_b
    row_b[x] = sums_b
    exchange(line_b, line_b_recv, zl, in_line)
    for target in to_x:
        send(row_b.at[x], row_b.at[x], row_b_recv.at[x], target)

    odd = lax.rem(x, 2)

    def across_z(slots, slots_in, recv, source, source_in, source_recv, width):
        joined = source[at_xy].astype(F32)
        for slot, _, _, _ in in_xy:
            receive(source_in.at[slot], source_recv.at[slot])
            joined = joined + source_in[slot].astype(F32)
        for hi in range(NZH):
            at = width * hi
            mid = jnp.where(
                odd == 1, joined[:, at + 64 : at + 64 + width], joined[:, at : at + width]
            )
            for q in range(8):
                slots[hi * 8 + q, :, 0:width] = mid[q * 4 : (q + 1) * 4].astype(BF16)
                slots[hi * 8 + q, :, width:] = jnp.zeros((4, slots.shape[2] - width), BF16)
        for o, target in in_z:
            send(slots.at[o], slots_in.at[at_z], recv.at[at_z], target)

    scale = 1.0 / math.sqrt(131072)

    def at_last(slots, slots_in, recv, out):
        result = slots[at_z].astype(F32)
        for o, _ in in_z:
            receive(slots_in.at[o], recv.at[o])
            result = result + slots_in[o].astype(F32)
        out[...] = result * scale

    drain()
    across_z(zs, zs_in, zs_recv, s1, s1_in, s1_recv, 288)
    across_z(zt, zt_in, zt_recv, t1, t1_in, t1_recv, 96)
    for o in others_x:
        receive(row_b.at[o], row_b_recv.at[o])
    both = total(row_b, 4)
    deep_b[at_z] = jnp.where(y < 2, both[:, :HALF], both[:, HALF:])
    for _, target in in_z:
        send(deep_b.at[at_z], deep_b.at[at_z], deep_b_recv.at[at_z], target)

    gathered(line_b, line_b_recv, in_line)
    means = group_totals(total(line_b, 8) * gains) / (FRAMES_CELLS * (C // GROUPS))
    inner = (grad_white - means[1:2] - whitened * means[0:1]) * inv
    grad_latents[...] = (cot[...].astype(F32) + inner).astype(BF16)

    at_last(zs, zs_in, zs_recv, s_out)
    for o, _ in in_z:
        receive(deep_b.at[o], deep_b_recv.at[o])
    norm_out[...] = total(deep_b, 16) * scale
    at_last(zt, zt_in, zt_recv, t_out)
    drain()


MAIN_OUTS = (
    ((ROWS, C), BF16), ((ROWS, C), BF16), ((4, 384), F32), ((4, 128), F32), ((2, HALF), F32),
)


def main(lat, cot, ws, wt, gain, bias):
    hbm = pl.BlockSpec(memory_space=pltpu.HBM)
    dma = pltpu.SemaphoreType.DMA
    V = pltpu.VMEM
    return pl.pallas_call(
        main_kernel,
        name="main",
        out_shape=[jax.ShapeDtypeStruct(*shape) for shape in MAIN_OUTS],
        in_specs=[hbm] * 6,
        out_specs=[pl.BlockSpec(memory_space=pltpu.VMEM)] * 5,
        scratch_shapes=[
            V((6, ROWS, C), BF16), V((1, C), F32), V((1, C), F32),
            V((8 * 36, 8, C), BF16), V((8 * 12, 8, C), BF16),
            V((8, 2, C), F32), V((8, 2, C), F32), V((8, 2, C), F32), V((8, 2, C), F32),
            V((NX, 2, C), F32), V((16, 2, HALF), F32),
            V((3 * ROWS, 9 * C), BF16), V((3 * ROWS, C), BF16), V((2 * ROWS, 3 * C), BF16),
            V((2 * ROWS, C), BF16), V((ROWS, 9 * C), BF16), V((HALF, 2 * ROWS), BF16),
            V((16, 32, S_WIN), BF16), V((16, 32, S_WIN), BF16),
            V((16, 32, T_WIN), BF16), V((16, 32, T_WIN), BF16),
            V((16, 4, 384), BF16), V((16, 4, 384), BF16),
            V((16, 4, 128), BF16), V((16, 4, 128), BF16),
            dma((6,)), dma((SENDS,)),
            dma((8,)), dma((8,)), dma((8,)), dma((8,)), dma((4,)), dma((16,)),
            dma((2,)), dma((1,)), dma((1,)), dma((4,)), dma((1,)), dma((16,)),
            dma((4,)), dma((1,)), dma((16,)), dma((4,)), dma((4,)),
            dma((16,)), dma((16,)), dma((16,)), dma((16,)),
        ],
        compiler_params=pltpu.CompilerParams(
            collective_id=1, has_side_effects=True, vmem_limit_bytes=VMEM_BYTES
        ),
    )(*[pltpu.with_memory_space_constraint(a, pltpu.HBM) for a in (lat, cot, ws, wt, gain, bias)])


def finish_kernel(
    block_out, grad_latents, sums_s, sums_t, norms,
    out_hbm, latents_hbm, spatial_hbm, temporal_hbm, norm_hbm,
    spatial, temporal, norm, store_sem,
):
    wide = lax.axis_index("wide")
    stores = [
        pltpu.make_async_copy(source, target, store_sem.at[k])
        for k, (source, target) in enumerate(
            (
                (block_out, out_hbm),
                (grad_latents, latents_hbm),
                (spatial, spatial_hbm),
                (temporal, temporal_hbm),
                (norm, norm_hbm),
            )
        )
    ]
    stores[0].start()
    stores[1].start()
    spatial[...] = sums_s[:, :288]
    stores[2].start()
    temporal[...] = sums_t[:, :96]
    stores[3].start()
    lane = lax.broadcasted_iota(jnp.int32, (2, HALF), 1)
    for k in range(4):
        norm[:, k : k + 1] = jnp.sum(
            jnp.where(lane == lax.rem(4 * wide, HALF) + k, norms[...], 0.0), axis=1, keepdims=True
        )
    stores[4].start()
    for copy in stores:
        copy.wait()


def finish(*parts):
    hbm = pl.BlockSpec(memory_space=pltpu.HBM)
    dma = pltpu.SemaphoreType.DMA
    last = [((4, 288), F32), ((4, 96), F32), ((2, 4), F32)]
    return pl.pallas_call(
        finish_kernel,
        name="finish",
        out_shape=[jax.ShapeDtypeStruct(*shape) for shape in list(MAIN_OUTS[:2]) + last],
        in_specs=[pl.BlockSpec(memory_space=pltpu.VMEM)] * 5,
        out_specs=[hbm] * 5,
        scratch_shapes=[pltpu.VMEM(*shape) for shape in last] + [dma((5,))],
        compiler_params=pltpu.CompilerParams(vmem_limit_bytes=2 << 20),
    )(*parts)


def local(latents, cotangent, norm_gain, norm_bias, w_spatial, w_temporal):
    block_out, grad_latents, spatial, temporal, norm = finish(
        *main(
            latents.reshape(ROWS, C),
            cotangent.reshape(ROWS, C),
            w_spatial.reshape(36, 8, C),
            w_temporal.reshape(12, 8, C),
            norm_gain.reshape(1, C),
            norm_bias.reshape(1, C),
        )
    )
    return (
        block_out.reshape(latents.shape),
        grad_latents.reshape(latents.shape),
        spatial.T,
        temporal.T,
        norm,
    )


def solution(mesh):
    return jax.shard_map(
        local,
        mesh=mesh,
        in_specs=(
            P("dp", "wide", None, None, None),
            P("dp", "wide", None, None, None),
            P(),
            P(),
            P("dp", None),
            P("dp", None),
        ),
        out_specs=(
            P("dp", "wide", None, None, None),
            P("dp", "wide", None, None, None),
            P("dp", "wide"),
            P("dp", "wide"),
            P(None, "wide"),
        ),
        check_vma=False,
    )
```

```python
import math

import jax
import jax.numpy as jnp
from jax import lax
from jax.experimental import pallas as pl
from jax.experimental.pallas import tpu as pltpu
from jax.sharding import PartitionSpec as P

MESH = pl.DeviceIdType.MESH
F32 = jnp.float32
BF16 = jnp.bfloat16
GROUPS = 32
EPSILON = 1e-05
C = 256
CELLS = 128
COLS = 16
ROWS = 256
NX, NZH, NY, NZL, NC = 4, 2, 4, 8, 2
S_TILES, T_TILES = 4, 1
HALF = 128


def coords():
    dp, wide = lax.axis_index("dp"), lax.axis_index("wide")
    return (
        lax.div(dp, 2),
        lax.rem(dp, 2),
        lax.div(wide, 16),
        lax.rem(lax.div(wide, 2), 8),
        lax.rem(wide, 2),
    )


def device(x, zh, y, zl, c):
    return (x * 2 + zh, (y * 8 + zl) * 2 + c)


def remote(src, dst, send_sem, recv_sem, target):
    return pltpu.make_async_remote_copy(
        src_ref=src,
        dst_ref=dst,
        send_sem=send_sem,
        recv_sem=recv_sem,
        device_id=target,
        device_id_type=MESH,
    )


def greet(targets):
    barrier = pltpu.get_barrier_semaphore()
    for target in targets:
        pl.semaphore_signal(barrier, inc=1, device_id=target, device_id_type=MESH)
    return lambda: pl.semaphore_wait(barrier, len(targets))


def plane_peers(x, zh, y, zl, c):
    mine = y * 2 + c
    peers = []
    for k in range(1, 8):
        other = lax.rem(mine + k, 8)
        peers.append((other, device(x, zh, lax.div(other, 2), zl, lax.rem(other, 2))))
    return mine, peers


def line_peers(x, zh, y, zl, c):
    peers = []
    for k in range(1, 8):
        other = lax.rem(zl + k, 8)
        peers.append((other, device(x, zh, y, other, c)))
    return zl, peers


def total(slots, count):
    result = slots[0]
    for k in range(1, count):
        result = result + slots[k]
    return result


def group_ones():
    row = lax.broadcasted_iota(jnp.int32, (C, C), 0)
    col = lax.broadcasted_iota(jnp.int32, (C, C), 1)
    return (lax.div(row, C // GROUPS) == lax.div(col, C // GROUPS)).astype(F32)


def group_totals(two_rows):
    padded = jnp.concatenate([two_rows, jnp.zeros((6, C), F32)], axis=0)
    return jnp.dot(
        padded, group_ones(), precision=lax.Precision.HIGHEST, preferred_element_type=F32
    )


def column_iota(rows):
    return lax.rem(lax.broadcasted_iota(jnp.int32, (rows, C), 0), COLS)


def shifted(values, step):
    rows = values.shape[0]
    if step == 0:
        return values.astype(BF16)
    col = column_iota(rows)
    moved = pltpu.roll(values, (rows - step) % rows, 0)
    edge = COLS - 1 if step == 1 else 0
    return jnp.where(col == edge, 0.0, moved).astype(BF16)


def fill_windows(target, values, sign):
    frames = values.shape[0] // CELLS
    for dx in range(3):
        cols = shifted(values, sign * (dx - 1))
        for dy in range(3):
            step = sign * (dy - 1)
            lanes = pl.ds((3 * dy + dx) * C, C)
            if step == 0:
                target[:, lanes] = cols
                continue
            for frame in range(frames):
                base = frame * CELLS
                if step == 1:
                    target[base : base + CELLS - COLS, lanes] = cols[base + COLS : base + CELLS]
                    target[base + CELLS - COLS : base + CELLS, lanes] = jnp.zeros((COLS, C), BF16)
                else:
                    target[base + COLS : base + CELLS, lanes] = cols[base : base + CELLS - COLS]
                    target[base : base + COLS, lanes] = jnp.zeros((COLS, C), BF16)


def permutation(c):
    row = lax.broadcasted_iota(jnp.int32, (HALF, C), 0)
    col = lax.broadcasted_iota(jnp.int32, (HALF, C), 1)
    y, zl, j = lax.div(row, 32), lax.rem(lax.div(row, 4), 8), lax.rem(row, 4)
    return (col == y * 64 + zl * 8 + c * 4 + j).astype(F32).astype(BF16)


def times_transpose(left, right):
    return lax.dot_general(left, right, (((1,), (1,)), ((), ())), preferred_element_type=F32)


FRAMES_CELLS = 128 * CELLS


SENDS = 160
VMEM_BYTES = 40 << 20


def main_kernel(
    lat_hbm, cot_hbm, ws_hbm, wt_hbm, gain_hbm, bias_hbm,
    block_out, grad_latents, s_out, t_out, norm_out,
    frames, gain, bias, wsp, wtm,
    plane, line, plane_b, line_b, row_b, deep_b,
    windows, spatial, mixed, grad_act, adjoint, cot_t,
    s1, s1_in, t1, t1_in, zs, zs_in, zt, zt_in,
    local_sem, send_sem,
    plane_recv, line_recv, plane_b_recv, line_b_recv, row_b_recv, deep_b_recv,
    mate_recv, halo_recv, pass_recv, tx_recv, tz_recv, txy_recv,
    sx_recv, sz_recv, sxy_recv, c1_recv, c2_recv, s1_recv, t1_recv, zs_recv, zt_recv,
):
    x, zh, y, zl, c = coords()
    wide, dp = lax.axis_index("wide"), lax.axis_index("dp")
    lat_at, cot_at, edge_out, edge_in = 1 + c, 3 + c, 3 - c, 5 - 5 * c
    lat, cot = frames.at[lat_at], frames.at[cot_at]
    mine, in_plane = plane_peers(x, zh, y, zl, c)
    _, in_line = line_peers(x, zh, y, zl, c)
    others_x = [lax.rem(x + k, NX) for k in (1, 2, 3)]
    to_x = [device(o, zh, y, zl, c) for o in others_x]
    to_c = device(x, zh, y, zl, 1 - c)
    to_far = device(x, 1 - zh, y, lax.rem(zl + 4, 8), c)
    ahead, behind = (dp, lax.rem(wide + 2, 64)), (dp, lax.rem(wide + 62, 64))
    edge_to = (dp, lax.rem(wide + 62 + 4 * c, 64))
    at_xy = x * 4 + y
    in_xy = []
    for k in range(1, 16):
        ox, oy = lax.rem(x + k // 4, NX), lax.rem(y + k % 4, NY)
        in_xy.append((ox * 4 + oy, device(ox, zh, oy, zl, c), ox, oy))
    at_z = zh * 8 + zl
    in_z = []
    for k in range(1, 16):
        o = lax.rem(at_z + k, 16)
        in_z.append((o, device(x, lax.div(o, 8), y, lax.rem(o, 8), c)))
    arrived = greet(
        [p for _, p in in_line]
        + [to_far, ahead, behind]
        + [in_xy[k - 1][1] for k in range(4, 16)]
        + [p for _, p in in_plane]
    )

    loads = [
        pltpu.make_async_copy(source, target, local_sem.at[k])
        for k, (source, target) in enumerate(
            (
                (lat_hbm, lat),
                (wt_hbm, wtm.at[pl.ds(12 * dp, 12)]),
                (ws_hbm, wsp.at[pl.ds(36 * dp, 36)]),
                (cot_hbm, cot),
                (gain_hbm, gain),
                (bias_hbm, bias),
            )
        )
    ]
    for copy in loads:
        copy.start()

    pending = []

    def send(ref, target, recv, where):
        copy = remote(ref, target, send_sem.at[len(pending)], recv, where)
        copy.start()
        pending.append(copy)

    drained = [0]

    def drain():
        for copy in pending[drained[0] :]:
            copy.wait_send()
        drained[0] = len(pending)

    def receive(ref, recv):
        remote(ref, ref, send_sem.at[0], recv, to_c).wait_recv()

    def exchange(slots, recv, at, peers):
        for _, target in peers:
            send(slots.at[at], slots.at[at], recv.at[at], target)

    def gathered(slots, recv, peers):
        for other, _ in peers:
            receive(slots.at[other], recv.at[other])

    loads[0].wait()
    wide_lat = lat[...].astype(F32)
    plane[mine, 0:1, :] = jnp.sum(wide_lat, axis=0, keepdims=True)
    plane[mine, 1:2, :] = jnp.sum(wide_lat * wide_lat, axis=0, keepdims=True)
    for copy in loads[1:]:
        copy.wait()
    arrived()

    def t_shard(hi, at):
        return wtm.at[pl.ds(12 * (2 * at + hi), 12)]

    def t_piece(at, quarter):
        return wtm.at[pl.ds(12 * (2 * at + 1 - zh) + 3 * quarter, 3)]

    def s_shard(hi, at, lanes):
        return wsp.at[pl.ds(36 * (2 * at + hi), 36), :, lanes]

    def s_piece(at, quarter, lanes):
        return wsp.at[pl.ds(36 * (2 * at + 1 - zh) + 9 * quarter, 9), :, lanes]

    part = wtm.at[pl.ds(12 * dp + 3 * y, 3)]
    send(part, part, tz_recv.at[0], to_far)
    exchange(plane, plane_recv, mine, in_plane)
    lanes = pl.ds(pl.multiple_of(c * HALF, HALF), HALF)
    part = wsp.at[pl.ds(36 * dp + 9 * y, 9), :, lanes]
    send(part, part, sz_recv.at[0], to_far)
    for target in to_x:
        send(t_shard(zh, x), t_shard(zh, x), tx_recv.at[x], target)
    send(lat, lat, mate_recv.at[0], to_c)
    send(cot, cot, mate_recv.at[1], to_c)
    send(frames.at[edge_out], frames.at[edge_in], halo_recv.at[0], edge_to)
    part = s_shard(zh, x, lanes)
    for target in to_x:
        send(part, part, sx_recv.at[x], target)

    gathered(plane, plane_recv, in_plane)
    line[zl] = total(plane, 8)
    exchange(line, line_recv, zl, in_line)

    part = t_piece(x, y)
    receive(part, tz_recv.at[0])
    for _, target, _, _ in in_xy:
        send(part, part, txy_recv.at[at_xy], target)
    part = s_piece(x, y, lanes)
    receive(part, sz_recv.at[0])
    for _, target, _, _ in in_xy:
        send(part, part, sxy_recv.at[at_xy], target)
    receive(frames.at[edge_in], halo_recv.at[0])
    send(frames.at[edge_in], frames.at[edge_in], pass_recv.at[0], to_c)
    for o in others_x:
        part = s_shard(zh, o, lanes)
        receive(part, sx_recv.at[o])
        send(part, part, c1_recv.at[o], to_c)
    receive(frames.at[2 - c], mate_recv.at[0])
    receive(frames.at[4 - c], mate_recv.at[1])
    order = permutation(c)
    for k in range(2):
        cot_t[:, k * ROWS : (k + 1) * ROWS] = times_transpose(order, frames[3 + k]).astype(BF16)

    gathered(line, line_recv, in_line)
    sums = group_totals(total(line, 8)) / (FRAMES_CELLS * (C // GROUPS))
    mean = sums[0:1]
    inv = 1.0 / jnp.sqrt(sums[1:2] - mean * mean + EPSILON)
    gains, biases = gain[...], bias[...]

    def normed_of(values):
        whitened = (values.astype(F32) - mean) * inv
        return whitened, whitened * gains + biases

    for k in (1, 2):
        _, normed = normed_of(frames[k])
        fill_windows(
            windows.at[k * ROWS : (k + 1) * ROWS, :], normed * jax.nn.sigmoid(normed), 1
        )

    receive(frames.at[5 * c], pass_recv.at[0])
    last = frames[5]
    later = jnp.where(wide < 62, last.astype(F32), 0.0).astype(BF16)
    for o in others_x:
        receive(t_shard(zh, o), tx_recv.at[o])
    for slot, _, ox, oy in in_xy:
        receive(t_piece(ox, oy), txy_recv.at[slot])
    held = jnp.concatenate([frames[3], frames[4], later], axis=0)
    running = jnp.zeros((2 * ROWS, C), F32)
    for delay in range(3):
        start = delay * CELLS
        running = running + times_transpose(
            held[start : start + 2 * ROWS], wtm[delay * 32 : (delay + 1) * 32].reshape(C, C)
        )
    grad_act[...] = running.astype(BF16)
    act_t = times_transpose(order, grad_act[...]).astype(BF16)

    def scatter(left, right, slots, slots_in, recv, tiles):
        for k in (1, 2, 3, 0):
            o = lax.rem(x + k, NX)
            odd_o = lax.rem(o, 2)
            first = lax.div((2 * tiles + 1) * o + 1, 2)
            whole = jnp.dot(
                left,
                right(pl.ds(pl.multiple_of(first * 128, 128), tiles * 128)),
                preferred_element_type=F32,
            ).astype(BF16)
            at_half = first + tiles - (tiles + 1) * odd_o
            half = jnp.dot(
                left, right(pl.ds(pl.multiple_of(at_half * 128, 128), 128)), preferred_element_type=F32
            )
            turned = pltpu.roll(half, 64, 1)
            low = jnp.where(odd_o == 1, turned, half)
            high = jnp.where(odd_o == 1, half, turned)
            left_half = lax.broadcasted_iota(jnp.int32, (16, 128), 1) < 64
            for p in range(NY):
                slot = o * 4 + p
                for tile in range(tiles):
                    slots[slot, tile * 32 : (tile + 1) * 32, :] = whole[
                        p * 32 : (p + 1) * 32, tile * 128 : (tile + 1) * 128
                    ]
                slots[slot, tiles * 32 :, :] = jnp.where(
                    left_half, low[p * 32 : p * 32 + 16], high[p * 32 + 16 : (p + 1) * 32]
                ).astype(BF16)
            for slot, target, _, _ in in_xy[max(4 * k - 1, 0) : 4 * k + 3]:
                send(slots.at[slot], slots_in.at[at_xy], recv.at[at_xy], target)

    def pass_weights(k, o):
        for slot, _, ox, oy in in_xy[max(4 * k - 1, 0) : 4 * k + 3]:
            receive(s_piece(ox, oy, lanes), sxy_recv.at[slot])
        part = s_shard(1 - zh, o, lanes)
        send(part, part, c2_recv.at[o], to_c)

    scatter(act_t, lambda at: windows[ROWS:, at], s1, s1_in, s1_recv, S_TILES)

    own_rows = pl.ds(pl.multiple_of(c * ROWS, ROWS), ROWS)
    fill_windows(adjoint, grad_act[own_rows, :].astype(F32), -1)
    _, normed = normed_of(frames[0])
    fill_windows(windows.at[0:ROWS, :], normed * jax.nn.sigmoid(normed), 1)

    for k in (1, 2, 3, 0):
        pass_weights(k, lax.rem(x + k, NX))
    other_lanes = pl.ds(pl.multiple_of((1 - c) * HALF, HALF), HALF)
    for o in others_x:
        receive(s_shard(zh, o, other_lanes), c1_recv.at[o])
    for o in range(NX):
        receive(s_shard(1 - zh, o, other_lanes), c2_recv.at[o])

    running = jnp.zeros((ROWS, C), F32)
    for tap in range(9):
        taps = slice(tap * C, (tap + 1) * C)
        running = running + times_transpose(
            adjoint[:, taps], wsp[tap * 32 : (tap + 1) * 32].reshape(C, C)
        )
    whitened, normed = normed_of(lat[...])
    sigmoid = jax.nn.sigmoid(normed)
    grad_normed = running * (sigmoid * (1.0 + normed * (1.0 - sigmoid)))
    plane_b[mine, 0:1, :] = jnp.sum(grad_normed * whitened, axis=0, keepdims=True)
    plane_b[mine, 1:2, :] = jnp.sum(grad_normed, axis=0, keepdims=True)
    exchange(plane_b, plane_b_recv, mine, in_plane)
    grad_white = grad_normed * gains

    conv = jnp.dot(windows[...], wsp[...].reshape(9 * C, C), preferred_element_type=F32)
    spatial[ROWS:, :] = conv[ROWS:].astype(BF16)
    spatial[:ROWS, :] = jnp.where(wide > 1, conv[:ROWS], 0.0).astype(BF16)
    for delay in range(3):
        start = (2 - delay) * CELLS
        mixed[:, delay * C : (delay + 1) * C] = spatial[start : start + 2 * ROWS, :]
    scatter(cot_t[...], lambda at: mixed[:, at], t1, t1_in, t1_recv, T_TILES)
    gathered(plane_b, plane_b_recv, in_plane)
    sums_b = total(plane_b, 8)
    line_b[zl] = sums_b
    row_b[x] = sums_b
    exchange(line_b, line_b_recv, zl, in_line)
    for target in to_x:
        send(row_b.at[x], row_b.at[x], row_b_recv.at[x], target)
    temporal = jnp.dot(
        mixed[own_rows, :], wtm[...].reshape(3 * C, C), preferred_element_type=F32
    )
    block_out[...] = (lat[...].astype(F32) + temporal).astype(BF16)


    odd = lax.rem(x, 2)

    def across_z(slots, slots_in, recv, source, source_in, source_recv, tiles, width):
        joined = source[at_xy].astype(F32)
        for slot, _, _, _ in in_xy:
            receive(source_in.at[slot], source_recv.at[slot])
            joined = joined + source_in[slot].astype(F32)
        whole = [joined[tile * 32 : (tile + 1) * 32] for tile in range(tiles)]
        fold = joined[tiles * 32 :]
        half = jnp.concatenate([fold[:, :64], fold[:, 64:]], axis=0)
        columns = jnp.where(
            odd == 1,
            jnp.concatenate([half] + whole, axis=1),
            jnp.concatenate(whole + [half], axis=1),
        )
        for hi in range(NZH):
            mid = columns[:, width * hi : width * (hi + 1)]
            for q in range(8):
                slots[hi * 8 + q, :, 0:width] = mid[q * 4 : (q + 1) * 4].astype(BF16)
                slots[hi * 8 + q, :, width:] = jnp.zeros((4, slots.shape[2] - width), BF16)
        for o, target in in_z:
            send(slots.at[o], slots_in.at[at_z], recv.at[at_z], target)

    scale = 1.0 / math.sqrt(131072)

    def at_last(slots, slots_in, recv, out):
        result = slots[at_z].astype(F32)
        for o, _ in in_z:
            receive(slots_in.at[o], recv.at[o])
            result = result + slots_in[o].astype(F32)
        out[...] = result * scale

    across_z(zs, zs_in, zs_recv, s1, s1_in, s1_recv, S_TILES, 288)
    across_z(zt, zt_in, zt_recv, t1, t1_in, t1_recv, T_TILES, 96)
    for o in others_x:
        receive(row_b.at[o], row_b_recv.at[o])
    both = total(row_b, 4)
    deep_b[at_z] = jnp.where(y < 2, both[:, :HALF], both[:, HALF:])
    for _, target in in_z:
        send(deep_b.at[at_z], deep_b.at[at_z], deep_b_recv.at[at_z], target)

    drain()
    gathered(line_b, line_b_recv, in_line)
    means = group_totals(total(line_b, 8) * gains) / (FRAMES_CELLS * (C // GROUPS))
    inner = (grad_white - means[1:2] - whitened * means[0:1]) * inv
    grad_latents[...] = (cot[...].astype(F32) + inner).astype(BF16)

    at_last(zs, zs_in, zs_recv, s_out)
    for o, _ in in_z:
        receive(deep_b.at[o], deep_b_recv.at[o])
    norm_out[...] = total(deep_b, 16) * scale
    at_last(zt, zt_in, zt_recv, t_out)
    drain()


MAIN_OUTS = (
    ((ROWS, C), BF16), ((ROWS, C), BF16), ((4, 384), F32), ((4, 128), F32), ((2, HALF), F32),
)


def main(lat, cot, ws, wt, gain, bias):
    hbm = pl.BlockSpec(memory_space=pltpu.HBM)
    dma = pltpu.SemaphoreType.DMA
    V = pltpu.VMEM
    return pl.pallas_call(
        main_kernel,
        name="main",
        out_shape=[jax.ShapeDtypeStruct(*shape) for shape in MAIN_OUTS],
        in_specs=[hbm] * 6,
        out_specs=[pl.BlockSpec(memory_space=pltpu.VMEM)] * 5,
        scratch_shapes=[
            V((6, ROWS, C), BF16), V((1, C), F32), V((1, C), F32),
            V((8 * 36, 8, C), BF16), V((8 * 12, 8, C), BF16),
            V((8, 2, C), F32), V((8, 2, C), F32), V((8, 2, C), F32), V((8, 2, C), F32),
            V((NX, 2, C), F32), V((16, 2, HALF), F32),
            V((3 * ROWS, 9 * C), BF16), V((3 * ROWS, C), BF16), V((2 * ROWS, 3 * C), BF16),
            V((2 * ROWS, C), BF16), V((ROWS, 9 * C), BF16), V((HALF, 2 * ROWS), BF16),
            V((16, 32 * S_TILES + 16, 128), BF16), V((16, 32 * S_TILES + 16, 128), BF16),
            V((16, 32 * T_TILES + 16, 128), BF16), V((16, 32 * T_TILES + 16, 128), BF16),
            V((16, 4, 384), BF16), V((16, 4, 384), BF16),
            V((16, 4, 128), BF16), V((16, 4, 128), BF16),
            dma((6,)), dma((SENDS,)),
            dma((8,)), dma((8,)), dma((8,)), dma((8,)), dma((4,)), dma((16,)),
            dma((2,)), dma((1,)), dma((1,)), dma((4,)), dma((1,)), dma((16,)),
            dma((4,)), dma((1,)), dma((16,)), dma((4,)), dma((4,)),
            dma((16,)), dma((16,)), dma((16,)), dma((16,)),
        ],
        compiler_params=pltpu.CompilerParams(
            collective_id=1, has_side_effects=True, vmem_limit_bytes=VMEM_BYTES
        ),
    )(*[pltpu.with_memory_space_constraint(a, pltpu.HBM) for a in (lat, cot, ws, wt, gain, bias)])


def finish_kernel(
    block_out, grad_latents, sums_s, sums_t, norms,
    out_hbm, latents_hbm, spatial_hbm, temporal_hbm, norm_hbm,
    spatial, temporal, norm, store_sem,
):
    wide = lax.axis_index("wide")
    stores = [
        pltpu.make_async_copy(source, target, store_sem.at[k])
        for k, (source, target) in enumerate(
            (
                (block_out, out_hbm),
                (grad_latents, latents_hbm),
                (spatial, spatial_hbm),
                (temporal, temporal_hbm),
                (norm, norm_hbm),
            )
        )
    ]
    stores[0].start()
    stores[1].start()
    spatial[...] = sums_s[:, :288]
    stores[2].start()
    temporal[...] = sums_t[:, :96]
    stores[3].start()
    lane = lax.broadcasted_iota(jnp.int32, (2, HALF), 1)
    for k in range(4):
        norm[:, k : k + 1] = jnp.sum(
            jnp.where(lane == lax.rem(4 * wide, HALF) + k, norms[...], 0.0), axis=1, keepdims=True
        )
    stores[4].start()
    for copy in stores:
        copy.wait()


def finish(*parts):
    hbm = pl.BlockSpec(memory_space=pltpu.HBM)
    dma = pltpu.SemaphoreType.DMA
    last = [((4, 288), F32), ((4, 96), F32), ((2, 4), F32)]
    return pl.pallas_call(
        finish_kernel,
        name="finish",
        out_shape=[jax.ShapeDtypeStruct(*shape) for shape in list(MAIN_OUTS[:2]) + last],
        in_specs=[pl.BlockSpec(memory_space=pltpu.VMEM)] * 5,
        out_specs=[hbm] * 5,
        scratch_shapes=[pltpu.VMEM(*shape) for shape in last] + [dma((5,))],
        compiler_params=pltpu.CompilerParams(vmem_limit_bytes=2 << 20),
    )(*parts)


def local(latents, cotangent, norm_gain, norm_bias, w_spatial, w_temporal):
    block_out, grad_latents, spatial, temporal, norm = finish(
        *main(
            latents.reshape(ROWS, C),
            cotangent.reshape(ROWS, C),
            w_spatial.reshape(36, 8, C),
            w_temporal.reshape(12, 8, C),
            norm_gain.reshape(1, C),
            norm_bias.reshape(1, C),
        )
    )
    return (
        block_out.reshape(latents.shape),
        grad_latents.reshape(latents.shape),
        spatial.T,
        temporal.T,
        norm,
    )


def solution(mesh):
    return jax.shard_map(
        local,
        mesh=mesh,
        in_specs=(
            P("dp", "wide", None, None, None),
            P("dp", "wide", None, None, None),
            P(),
            P(),
            P("dp", None),
            P("dp", None),
        ),
        out_specs=(
            P("dp", "wide", None, None, None),
            P("dp", "wide", None, None, None),
            P("dp", "wide"),
            P("dp", "wide"),
            P(None, "wide"),
        ),
        check_vma=False,
    )
```

```python
import math

import jax
import jax.numpy as jnp
from jax import lax
from jax.experimental import pallas as pl
from jax.experimental.pallas import tpu as pltpu
from jax.sharding import PartitionSpec as P

MESH = pl.DeviceIdType.MESH
F32 = jnp.float32
BF16 = jnp.bfloat16
GROUPS = 32
EPSILON = 1e-05
C = 256
CELLS = 128
COLS = 16
ROWS = 256
NX, NZH, NY, NZL, NC = 4, 2, 4, 8, 2
S_TILES, T_TILES = 4, 1
HALF = 128


def coords():
    dp, wide = lax.axis_index("dp"), lax.axis_index("wide")
    return (
        lax.div(dp, 2),
        lax.rem(dp, 2),
        lax.div(wide, 16),
        lax.rem(lax.div(wide, 2), 8),
        lax.rem(wide, 2),
    )


def device(x, zh, y, zl, c):
    return (x * 2 + zh, (y * 8 + zl) * 2 + c)


def remote(src, dst, send_sem, recv_sem, target):
    return pltpu.make_async_remote_copy(
        src_ref=src,
        dst_ref=dst,
        send_sem=send_sem,
        recv_sem=recv_sem,
        device_id=target,
        device_id_type=MESH,
    )


def greet(targets):
    barrier = pltpu.get_barrier_semaphore()
    for target in targets:
        pl.semaphore_signal(barrier, inc=1, device_id=target, device_id_type=MESH)
    return lambda: pl.semaphore_wait(barrier, len(targets))


def plane_peers(x, zh, y, zl, c):
    mine = y * 2 + c
    peers = []
    for k in range(1, 8):
        other = lax.rem(mine + k, 8)
        peers.append((other, device(x, zh, lax.div(other, 2), zl, lax.rem(other, 2))))
    return mine, peers


def line_peers(x, zh, y, zl, c):
    peers = []
    for k in range(1, 8):
        other = lax.rem(zl + k, 8)
        peers.append((other, device(x, zh, y, other, c)))
    return zl, peers


def total(slots, count):
    result = slots[0]
    for k in range(1, count):
        result = result + slots[k]
    return result


def group_ones():
    row = lax.broadcasted_iota(jnp.int32, (C, C), 0)
    col = lax.broadcasted_iota(jnp.int32, (C, C), 1)
    return (lax.div(row, C // GROUPS) == lax.div(col, C // GROUPS)).astype(F32)


def group_totals(two_rows):
    padded = jnp.concatenate([two_rows, jnp.zeros((6, C), F32)], axis=0)
    return jnp.dot(
        padded, group_ones(), precision=lax.Precision.HIGHEST, preferred_element_type=F32
    )


def column_iota(rows):
    return lax.rem(lax.broadcasted_iota(jnp.int32, (rows, C), 0), COLS)


def shifted(values, step):
    rows = values.shape[0]
    if step == 0:
        return values.astype(BF16)
    col = column_iota(rows)
    moved = pltpu.roll(values, (rows - step) % rows, 0)
    edge = COLS - 1 if step == 1 else 0
    return jnp.where(col == edge, 0.0, moved).astype(BF16)


def fill_windows(target, values, sign):
    frames = values.shape[0] // CELLS
    for dx in range(3):
        cols = shifted(values, sign * (dx - 1))
        for dy in range(3):
            step = sign * (dy - 1)
            lanes = pl.ds((3 * dy + dx) * C, C)
            if step == 0:
                target[:, lanes] = cols
                continue
            for frame in range(frames):
                base = frame * CELLS
                if step == 1:
                    target[base : base + CELLS - COLS, lanes] = cols[base + COLS : base + CELLS]
                    target[base + CELLS - COLS : base + CELLS, lanes] = jnp.zeros((COLS, C), BF16)
                else:
                    target[base + COLS : base + CELLS, lanes] = cols[base : base + CELLS - COLS]
                    target[base : base + COLS, lanes] = jnp.zeros((COLS, C), BF16)


def permutation(c):
    row = lax.broadcasted_iota(jnp.int32, (HALF, C), 0)
    col = lax.broadcasted_iota(jnp.int32, (HALF, C), 1)
    y, zl, j = lax.div(row, 32), lax.rem(lax.div(row, 4), 8), lax.rem(row, 4)
    return (col == y * 64 + zl * 8 + c * 4 + j).astype(F32).astype(BF16)


def times_transpose(left, right):
    return lax.dot_general(left, right, (((1,), (1,)), ((), ())), preferred_element_type=F32)


FRAMES_CELLS = 128 * CELLS


SENDS = 160
VMEM_BYTES = 40 << 20


def main_kernel(
    lat_hbm, cot_hbm, ws_hbm, wt_hbm, gain_hbm, bias_hbm,
    block_out, grad_latents, s_out, t_out, norm_out,
    frames, gain, bias, wsp, wtm,
    plane, line, plane_b, line_b, row_b, deep_b,
    windows, spatial, mixed, grad_act, adjoint, cot_t,
    s1, s1_in, t1, t1_in, zs, zs_in, zt, zt_in,
    local_sem, send_sem,
    plane_recv, line_recv, plane_b_recv, line_b_recv, row_b_recv, deep_b_recv,
    mate_recv, halo_recv, pass_recv, tx_recv, tz_recv, txy_recv,
    sx_recv, sz_recv, sxy_recv, c1_recv, c2_recv, s1_recv, t1_recv, zs_recv, zt_recv,
):
    x, zh, y, zl, c = coords()
    wide, dp = lax.axis_index("wide"), lax.axis_index("dp")
    lat_at, cot_at, edge_out, edge_in = 1 + c, 3 + c, 3 - c, 5 - 5 * c
    lat, cot = frames.at[lat_at], frames.at[cot_at]
    mine, in_plane = plane_peers(x, zh, y, zl, c)
    _, in_line = line_peers(x, zh, y, zl, c)
    others_x = [lax.rem(x + k, NX) for k in (1, 2, 3)]
    to_x = [device(o, zh, y, zl, c) for o in others_x]
    to_c = device(x, zh, y, zl, 1 - c)
    to_far = device(x, 1 - zh, y, lax.rem(zl + 4, 8), c)
    ahead, behind = (dp, lax.rem(wide + 2, 64)), (dp, lax.rem(wide + 62, 64))
    edge_to = (dp, lax.rem(wide + 62 + 4 * c, 64))
    at_xy = x * 4 + y
    in_xy = []
    for kx in range(NX):
        for ky in (2, 1, 3, 0):
            if kx + ky:
                ox, oy = lax.rem(x + kx, NX), lax.rem(y + ky, NY)
                in_xy.append((ox * 4 + oy, device(ox, zh, oy, zl, c), ox, oy))
    at_z = zh * 8 + zl
    in_z = []
    for k in (8, 7, 9, 6, 10, 5, 11, 4, 12, 3, 13, 2, 14, 1, 15):
        o = lax.rem(at_z + k, 16)
        in_z.append((o, device(x, lax.div(o, 8), y, lax.rem(o, 8), c)))
    arrived = greet(
        [p for _, p in in_line]
        + [to_far, ahead, behind]
        + [in_xy[k - 1][1] for k in range(4, 16)]
        + [p for _, p in in_plane]
    )

    loads = [
        pltpu.make_async_copy(source, target, local_sem.at[k])
        for k, (source, target) in enumerate(
            (
                (lat_hbm, lat),
                (wt_hbm, wtm.at[pl.ds(12 * dp, 12)]),
                (ws_hbm, wsp.at[pl.ds(36 * dp, 36)]),
                (cot_hbm, cot),
                (gain_hbm, gain),
                (bias_hbm, bias),
            )
        )
    ]
    for copy in loads:
        copy.start()

    pending = []

    def send(ref, target, recv, where):
        copy = remote(ref, target, send_sem.at[len(pending)], recv, where)
        copy.start()
        pending.append(copy)

    drained = [0]

    def drain():
        for copy in pending[drained[0] :]:
            copy.wait_send()
        drained[0] = len(pending)

    def receive(ref, recv):
        remote(ref, ref, send_sem.at[0], recv, to_c).wait_recv()

    def exchange(slots, recv, at, peers):
        for _, target in peers:
            send(slots.at[at], slots.at[at], recv.at[at], target)

    def gathered(slots, recv, peers):
        for other, _ in peers:
            receive(slots.at[other], recv.at[other])

    loads[0].wait()
    wide_lat = lat[...].astype(F32)
    plane[mine, 0:1, :] = jnp.sum(wide_lat, axis=0, keepdims=True)
    plane[mine, 1:2, :] = jnp.sum(wide_lat * wide_lat, axis=0, keepdims=True)
    for copy in loads[1:]:
        copy.wait()
    arrived()

    def t_shard(hi, at):
        return wtm.at[pl.ds(12 * (2 * at + hi), 12)]

    def t_piece(at, quarter):
        return wtm.at[pl.ds(12 * (2 * at + 1 - zh) + 3 * quarter, 3)]

    def s_shard(hi, at, lanes):
        return wsp.at[pl.ds(36 * (2 * at + hi), 36), :, lanes]

    def s_piece(at, quarter, lanes):
        return wsp.at[pl.ds(36 * (2 * at + 1 - zh) + 9 * quarter, 9), :, lanes]

    part = wtm.at[pl.ds(12 * dp + 3 * y, 3)]
    send(part, part, tz_recv.at[0], to_far)
    exchange(plane, plane_recv, mine, in_plane)
    lanes = pl.ds(pl.multiple_of(c * HALF, HALF), HALF)
    part = wsp.at[pl.ds(36 * dp + 9 * y, 9), :, lanes]
    send(part, part, sz_recv.at[0], to_far)
    for target in to_x:
        send(t_shard(zh, x), t_shard(zh, x), tx_recv.at[x], target)
    send(lat, lat, mate_recv.at[0], to_c)
    send(cot, cot, mate_recv.at[1], to_c)
    send(frames.at[edge_out], frames.at[edge_in], halo_recv.at[0], edge_to)
    part = s_shard(zh, x, lanes)
    for target in to_x:
        send(part, part, sx_recv.at[x], target)

    gathered(plane, plane_recv, in_plane)
    line[zl] = total(plane, 8)
    exchange(line, line_recv, zl, in_line)

    part = t_piece(x, y)
    receive(part, tz_recv.at[0])
    for _, target, _, _ in in_xy:
        send(part, part, txy_recv.at[at_xy], target)
    part = s_piece(x, y, lanes)
    receive(part, sz_recv.at[0])
    for _, target, _, _ in in_xy:
        send(part, part, sxy_recv.at[at_xy], target)
    receive(frames.at[edge_in], halo_recv.at[0])
    send(frames.at[edge_in], frames.at[edge_in], pass_recv.at[0], to_c)
    for o in others_x:
        part = s_shard(zh, o, lanes)
        receive(part, sx_recv.at[o])
        send(part, part, c1_recv.at[o], to_c)
    receive(frames.at[2 - c], mate_recv.at[0])
    receive(frames.at[4 - c], mate_recv.at[1])
    order = permutation(c)
    for k in range(2):
        cot_t[:, k * ROWS : (k + 1) * ROWS] = times_transpose(order, frames[3 + k]).astype(BF16)

    gathered(line, line_recv, in_line)
    sums = group_totals(total(line, 8)) / (FRAMES_CELLS * (C // GROUPS))
    mean = sums[0:1]
    inv = 1.0 / jnp.sqrt(sums[1:2] - mean * mean + EPSILON)
    gains, biases = gain[...], bias[...]

    def normed_of(values):
        whitened = (values.astype(F32) - mean) * inv
        return whitened, whitened * gains + biases

    for k in (1, 2):
        _, normed = normed_of(frames[k])
        fill_windows(
            windows.at[k * ROWS : (k + 1) * ROWS, :], normed * jax.nn.sigmoid(normed), 1
        )

    receive(frames.at[5 * c], pass_recv.at[0])
    last = frames[5]
    later = jnp.where(wide < 62, last.astype(F32), 0.0).astype(BF16)
    for o in others_x:
        receive(t_shard(zh, o), tx_recv.at[o])
    for slot, _, ox, oy in in_xy:
        receive(t_piece(ox, oy), txy_recv.at[slot])
    held = jnp.concatenate([frames[3], frames[4], later], axis=0)
    running = jnp.zeros((2 * ROWS, C), F32)
    for delay in range(3):
        start = delay * CELLS
        running = running + times_transpose(
            held[start : start + 2 * ROWS], wtm[delay * 32 : (delay + 1) * 32].reshape(C, C)
        )
    grad_act[...] = running.astype(BF16)
    act_t = times_transpose(order, grad_act[...]).astype(BF16)

    def scatter(left, right, slots, slots_in, recv, tiles):
        for k in (2, 0, 1, 3):
            o = lax.rem(x + k, NX)
            odd_o = lax.rem(o, 2)
            first = lax.div((2 * tiles + 1) * o + 1, 2)
            whole = jnp.dot(
                left,
                right(pl.ds(pl.multiple_of(first * 128, 128), tiles * 128)),
                preferred_element_type=F32,
            ).astype(BF16)
            at_half = first + tiles - (tiles + 1) * odd_o
            half = jnp.dot(
                left, right(pl.ds(pl.multiple_of(at_half * 128, 128), 128)), preferred_element_type=F32
            )
            turned = pltpu.roll(half, 64, 1)
            low = jnp.where(odd_o == 1, turned, half)
            high = jnp.where(odd_o == 1, half, turned)
            left_half = lax.broadcasted_iota(jnp.int32, (16, 128), 1) < 64
            for p in range(NY):
                slot = o * 4 + p
                for tile in range(tiles):
                    slots[slot, tile * 32 : (tile + 1) * 32, :] = whole[
                        p * 32 : (p + 1) * 32, tile * 128 : (tile + 1) * 128
                    ]
                slots[slot, tiles * 32 :, :] = jnp.where(
                    left_half, low[p * 32 : p * 32 + 16], high[p * 32 + 16 : (p + 1) * 32]
                ).astype(BF16)
            for slot, target, _, _ in in_xy[max(4 * k - 1, 0) : 4 * k + 3]:
                send(slots.at[slot], slots_in.at[at_xy], recv.at[at_xy], target)

    def pass_weights(k, o):
        for slot, _, ox, oy in in_xy[max(4 * k - 1, 0) : 4 * k + 3]:
            receive(s_piece(ox, oy, lanes), sxy_recv.at[slot])
        part = s_shard(1 - zh, o, lanes)
        send(part, part, c2_recv.at[o], to_c)

    scatter(act_t, lambda at: windows[ROWS:, at], s1, s1_in, s1_recv, S_TILES)

    own_rows = pl.ds(pl.multiple_of(c * ROWS, ROWS), ROWS)
    fill_windows(adjoint, grad_act[own_rows, :].astype(F32), -1)
    _, normed = normed_of(frames[0])
    fill_windows(windows.at[0:ROWS, :], normed * jax.nn.sigmoid(normed), 1)

    for k in (1, 2, 3, 0):
        pass_weights(k, lax.rem(x + k, NX))
    other_lanes = pl.ds(pl.multiple_of((1 - c) * HALF, HALF), HALF)
    for o in others_x:
        receive(s_shard(zh, o, other_lanes), c1_recv.at[o])
    for o in range(NX):
        receive(s_shard(1 - zh, o, other_lanes), c2_recv.at[o])

    running = jnp.zeros((ROWS, C), F32)
    for tap in range(9):
        taps = slice(tap * C, (tap + 1) * C)
        running = running + times_transpose(
            adjoint[:, taps], wsp[tap * 32 : (tap + 1) * 32].reshape(C, C)
        )
    whitened, normed = normed_of(lat[...])
    sigmoid = jax.nn.sigmoid(normed)
    grad_normed = running * (sigmoid * (1.0 + normed * (1.0 - sigmoid)))
    plane_b[mine, 0:1, :] = jnp.sum(grad_normed * whitened, axis=0, keepdims=True)
    plane_b[mine, 1:2, :] = jnp.sum(grad_normed, axis=0, keepdims=True)
    exchange(plane_b, plane_b_recv, mine, in_plane)
    grad_white = grad_normed * gains

    conv = jnp.dot(windows[...], wsp[...].reshape(9 * C, C), preferred_element_type=F32)
    spatial[ROWS:, :] = conv[ROWS:].astype(BF16)
    spatial[:ROWS, :] = jnp.where(wide > 1, conv[:ROWS], 0.0).astype(BF16)
    for delay in range(3):
        start = (2 - delay) * CELLS
        mixed[:, delay * C : (delay + 1) * C] = spatial[start : start + 2 * ROWS, :]
    scatter(cot_t[...], lambda at: mixed[:, at], t1, t1_in, t1_recv, T_TILES)
    gathered(plane_b, plane_b_recv, in_plane)
    sums_b = total(plane_b, 8)
    line_b[zl] = sums_b
    row_b[x] = sums_b
    exchange(line_b, line_b_recv, zl, in_line)
    for target in to_x:
        send(row_b.at[x], row_b.at[x], row_b_recv.at[x], target)
    temporal = jnp.dot(
        mixed[own_rows, :], wtm[...].reshape(3 * C, C), preferred_element_type=F32
    )
    block_out[...] = (lat[...].astype(F32) + temporal).astype(BF16)


    odd = lax.rem(x, 2)

    def across_z(slots, slots_in, recv, source, source_in, source_recv, tiles, width):
        joined = source[at_xy].astype(F32)
        for slot, _, _, _ in in_xy:
            receive(source_in.at[slot], source_recv.at[slot])
            joined = joined + source_in[slot].astype(F32)
        whole = [joined[tile * 32 : (tile + 1) * 32] for tile in range(tiles)]
        fold = joined[tiles * 32 :]
        half = jnp.concatenate([fold[:, :64], fold[:, 64:]], axis=0)
        columns = jnp.where(
            odd == 1,
            jnp.concatenate([half] + whole, axis=1),
            jnp.concatenate(whole + [half], axis=1),
        )
        for hi in range(NZH):
            mid = columns[:, width * hi : width * (hi + 1)]
            for q in range(8):
                slots[hi * 8 + q, :, 0:width] = mid[q * 4 : (q + 1) * 4].astype(BF16)
                slots[hi * 8 + q, :, width:] = jnp.zeros((4, slots.shape[2] - width), BF16)
        for o, target in in_z:
            send(slots.at[o], slots_in.at[at_z], recv.at[at_z], target)

    scale = 1.0 / math.sqrt(131072)

    def at_last(slots, slots_in, recv, out):
        result = slots[at_z].astype(F32)
        for o, _ in in_z:
            receive(slots_in.at[o], recv.at[o])
            result = result + slots_in[o].astype(F32)
        out[...] = result * scale

    across_z(zs, zs_in, zs_recv, s1, s1_in, s1_recv, S_TILES, 288)
    across_z(zt, zt_in, zt_recv, t1, t1_in, t1_recv, T_TILES, 96)
    for o in others_x:
        receive(row_b.at[o], row_b_recv.at[o])
    both = total(row_b, 4)
    deep_b[at_z] = jnp.where(y < 2, both[:, :HALF], both[:, HALF:])
    for _, target in in_z:
        send(deep_b.at[at_z], deep_b.at[at_z], deep_b_recv.at[at_z], target)

    drain()
    gathered(line_b, line_b_recv, in_line)
    means = group_totals(total(line_b, 8) * gains) / (FRAMES_CELLS * (C // GROUPS))
    inner = (grad_white - means[1:2] - whitened * means[0:1]) * inv
    grad_latents[...] = (cot[...].astype(F32) + inner).astype(BF16)

    at_last(zs, zs_in, zs_recv, s_out)
    for o, _ in in_z:
        receive(deep_b.at[o], deep_b_recv.at[o])
    norm_out[...] = total(deep_b, 16) * scale
    at_last(zt, zt_in, zt_recv, t_out)
    drain()


MAIN_OUTS = (
    ((ROWS, C), BF16), ((ROWS, C), BF16), ((4, 384), F32), ((4, 128), F32), ((2, HALF), F32),
)


def main(lat, cot, ws, wt, gain, bias):
    hbm = pl.BlockSpec(memory_space=pltpu.HBM)
    dma = pltpu.SemaphoreType.DMA
    V = pltpu.VMEM
    return pl.pallas_call(
        main_kernel,
        name="main",
        out_shape=[jax.ShapeDtypeStruct(*shape) for shape in MAIN_OUTS],
        in_specs=[hbm] * 6,
        out_specs=[pl.BlockSpec(memory_space=pltpu.VMEM)] * 5,
        scratch_shapes=[
            V((6, ROWS, C), BF16), V((1, C), F32), V((1, C), F32),
            V((8 * 36, 8, C), BF16), V((8 * 12, 8, C), BF16),
            V((8, 2, C), F32), V((8, 2, C), F32), V((8, 2, C), F32), V((8, 2, C), F32),
            V((NX, 2, C), F32), V((16, 2, HALF), F32),
            V((3 * ROWS, 9 * C), BF16), V((3 * ROWS, C), BF16), V((2 * ROWS, 3 * C), BF16),
            V((2 * ROWS, C), BF16), V((ROWS, 9 * C), BF16), V((HALF, 2 * ROWS), BF16),
            V((16, 32 * S_TILES + 16, 128), BF16), V((16, 32 * S_TILES + 16, 128), BF16),
            V((16, 32 * T_TILES + 16, 128), BF16), V((16, 32 * T_TILES + 16, 128), BF16),
            V((16, 4, 384), BF16), V((16, 4, 384), BF16),
            V((16, 4, 128), BF16), V((16, 4, 128), BF16),
            dma((6,)), dma((SENDS,)),
            dma((8,)), dma((8,)), dma((8,)), dma((8,)), dma((4,)), dma((16,)),
            dma((2,)), dma((1,)), dma((1,)), dma((4,)), dma((1,)), dma((16,)),
            dma((4,)), dma((1,)), dma((16,)), dma((4,)), dma((4,)),
            dma((16,)), dma((16,)), dma((16,)), dma((16,)),
        ],
        compiler_params=pltpu.CompilerParams(
            collective_id=1, has_side_effects=True, vmem_limit_bytes=VMEM_BYTES
        ),
    )(*[pltpu.with_memory_space_constraint(a, pltpu.HBM) for a in (lat, cot, ws, wt, gain, bias)])


def finish_kernel(
    block_out, grad_latents, sums_s, sums_t, norms,
    out_hbm, latents_hbm, spatial_hbm, temporal_hbm, norm_hbm,
    spatial, temporal, norm, store_sem,
):
    wide = lax.axis_index("wide")
    stores = [
        pltpu.make_async_copy(source, target, store_sem.at[k])
        for k, (source, target) in enumerate(
            (
                (block_out, out_hbm),
                (grad_latents, latents_hbm),
                (spatial, spatial_hbm),
                (temporal, temporal_hbm),
                (norm, norm_hbm),
            )
        )
    ]
    stores[0].start()
    stores[1].start()
    spatial[...] = sums_s[:, :288]
    stores[2].start()
    temporal[...] = sums_t[:, :96]
    stores[3].start()
    lane = lax.broadcasted_iota(jnp.int32, (2, HALF), 1)
    for k in range(4):
        norm[:, k : k + 1] = jnp.sum(
            jnp.where(lane == lax.rem(4 * wide, HALF) + k, norms[...], 0.0), axis=1, keepdims=True
        )
    stores[4].start()
    for copy in stores:
        copy.wait()


def finish(*parts):
    hbm = pl.BlockSpec(memory_space=pltpu.HBM)
    dma = pltpu.SemaphoreType.DMA
    last = [((4, 288), F32), ((4, 96), F32), ((2, 4), F32)]
    return pl.pallas_call(
        finish_kernel,
        name="finish",
        out_shape=[jax.ShapeDtypeStruct(*shape) for shape in list(MAIN_OUTS[:2]) + last],
        in_specs=[pl.BlockSpec(memory_space=pltpu.VMEM)] * 5,
        out_specs=[hbm] * 5,
        scratch_shapes=[pltpu.VMEM(*shape) for shape in last] + [dma((5,))],
        compiler_params=pltpu.CompilerParams(vmem_limit_bytes=2 << 20),
    )(*parts)


def local(latents, cotangent, norm_gain, norm_bias, w_spatial, w_temporal):
    block_out, grad_latents, spatial, temporal, norm = finish(
        *main(
            latents.reshape(ROWS, C),
            cotangent.reshape(ROWS, C),
            w_spatial.reshape(36, 8, C),
            w_temporal.reshape(12, 8, C),
            norm_gain.reshape(1, C),
            norm_bias.reshape(1, C),
        )
    )
    return (
        block_out.reshape(latents.shape),
        grad_latents.reshape(latents.shape),
        spatial.T,
        temporal.T,
        norm,
    )


def solution(mesh):
    return jax.shard_map(
        local,
        mesh=mesh,
        in_specs=(
            P("dp", "wide", None, None, None),
            P("dp", "wide", None, None, None),
            P(),
            P(),
            P("dp", None),
            P("dp", None),
        ),
        out_specs=(
            P("dp", "wide", None, None, None),
            P("dp", "wide", None, None, None),
            P("dp", "wide"),
            P("dp", "wide"),
            P(None, "wide"),
        ),
        check_vma=False,
    )
```

```python
import math

import jax
import jax.numpy as jnp
from jax import lax
from jax.experimental import pallas as pl
from jax.experimental.pallas import tpu as pltpu
from jax.sharding import PartitionSpec as P

MESH = pl.DeviceIdType.MESH
F32 = jnp.float32
BF16 = jnp.bfloat16
GROUPS = 32
EPSILON = 1e-05
C = 256
CELLS = 128
COLS = 16
ROWS = 256
NX, NZH, NY, NZL, NC = 4, 2, 4, 8, 2
S_TILES, T_TILES = 4, 1
HALF = 128


def coords():
    dp, wide = lax.axis_index("dp"), lax.axis_index("wide")
    return (
        lax.div(dp, 2),
        lax.rem(dp, 2),
        lax.div(wide, 16),
        lax.rem(lax.div(wide, 2), 8),
        lax.rem(wide, 2),
    )


def device(x, zh, y, zl, c):
    return (x * 2 + zh, (y * 8 + zl) * 2 + c)


def remote(src, dst, send_sem, recv_sem, target):
    return pltpu.make_async_remote_copy(
        src_ref=src,
        dst_ref=dst,
        send_sem=send_sem,
        recv_sem=recv_sem,
        device_id=target,
        device_id_type=MESH,
    )


def greet(targets):
    barrier = pltpu.get_barrier_semaphore()
    for target in targets:
        pl.semaphore_signal(barrier, inc=1, device_id=target, device_id_type=MESH)
    return lambda: pl.semaphore_wait(barrier, len(targets))


def plane_peers(x, zh, y, zl, c):
    mine = y * 2 + c
    peers = []
    for k in range(1, 8):
        other = lax.rem(mine + k, 8)
        peers.append((other, device(x, zh, lax.div(other, 2), zl, lax.rem(other, 2))))
    return mine, peers


def line_peers(x, zh, y, zl, c):
    peers = []
    for k in range(1, 8):
        other = lax.rem(zl + k + (1 - lax.div(zl, 4)) * (8 - 2 * k), 8)
        peers.append((other, device(x, zh, y, other, c)))
    return zl, peers


def total(slots, count):
    result = slots[0]
    for k in range(1, count):
        result = result + slots[k]
    return result


def group_ones():
    row = lax.broadcasted_iota(jnp.int32, (C, C), 0)
    col = lax.broadcasted_iota(jnp.int32, (C, C), 1)
    return (lax.div(row, C // GROUPS) == lax.div(col, C // GROUPS)).astype(F32)


def group_totals(two_rows):
    padded = jnp.concatenate([two_rows, jnp.zeros((6, C), F32)], axis=0)
    return jnp.dot(
        padded, group_ones(), precision=lax.Precision.HIGHEST, preferred_element_type=F32
    )


def column_iota(rows):
    return lax.rem(lax.broadcasted_iota(jnp.int32, (rows, C), 0), COLS)


def shifted(values, step):
    rows = values.shape[0]
    if step == 0:
        return values.astype(BF16)
    col = column_iota(rows)
    moved = pltpu.roll(values, (rows - step) % rows, 0)
    edge = COLS - 1 if step == 1 else 0
    return jnp.where(col == edge, 0.0, moved).astype(BF16)


def fill_windows(target, values, sign):
    frames = values.shape[0] // CELLS
    for dx in range(3):
        cols = shifted(values, sign * (dx - 1))
        for dy in range(3):
            step = sign * (dy - 1)
            lanes = pl.ds((3 * dy + dx) * C, C)
            if step == 0:
                target[:, lanes] = cols
                continue
            for frame in range(frames):
                base = frame * CELLS
                if step == 1:
                    target[base : base + CELLS - COLS, lanes] = cols[base + COLS : base + CELLS]
                    target[base + CELLS - COLS : base + CELLS, lanes] = jnp.zeros((COLS, C), BF16)
                else:
                    target[base + COLS : base + CELLS, lanes] = cols[base : base + CELLS - COLS]
                    target[base : base + COLS, lanes] = jnp.zeros((COLS, C), BF16)


def permutation(c):
    row = lax.broadcasted_iota(jnp.int32, (HALF, C), 0)
    col = lax.broadcasted_iota(jnp.int32, (HALF, C), 1)
    y, zl, j = lax.div(row, 32), lax.rem(lax.div(row, 4), 8), lax.rem(row, 4)
    return (col == y * 64 + zl * 8 + c * 4 + j).astype(F32).astype(BF16)


def times_transpose(left, right):
    return lax.dot_general(left, right, (((1,), (1,)), ((), ())), preferred_element_type=F32)


FRAMES_CELLS = 128 * CELLS


SENDS = 160
VMEM_BYTES = 40 << 20


def main_kernel(
    lat_hbm, cot_hbm, ws_hbm, wt_hbm, gain_hbm, bias_hbm,
    block_out, grad_latents, s_out, t_out, norm_out,
    frames, gain, bias, wsp, wtm,
    plane, line, plane_b, line_b, row_b, deep_b,
    windows, spatial, mixed, grad_act, adjoint, cot_t,
    s1, s1_in, t1, t1_in, zs, zs_in, zt, zt_in,
    local_sem, send_sem,
    plane_recv, line_recv, plane_b_recv, line_b_recv, row_b_recv, deep_b_recv,
    mate_recv, halo_recv, pass_recv, tx_recv, tz_recv, txy_recv,
    sx_recv, sz_recv, sxy_recv, c1_recv, c2_recv, s1_recv, t1_recv, zs_recv, zt_recv,
):
    x, zh, y, zl, c = coords()
    wide, dp = lax.axis_index("wide"), lax.axis_index("dp")
    lat_at, cot_at, edge_out, edge_in = 1 + c, 3 + c, 3 - c, 5 - 5 * c
    lat, cot = frames.at[lat_at], frames.at[cot_at]
    mine, in_plane = plane_peers(x, zh, y, zl, c)
    _, in_line = line_peers(x, zh, y, zl, c)
    others_x = [lax.rem(x + k, NX) for k in (1, 2, 3)]
    to_x = [device(o, zh, y, zl, c) for o in others_x]
    to_c = device(x, zh, y, zl, 1 - c)
    to_far = device(x, 1 - zh, y, lax.rem(zl + 4, 8), c)
    ahead, behind = (dp, lax.rem(wide + 2, 64)), (dp, lax.rem(wide + 62, 64))
    edge_to = (dp, lax.rem(wide + 62 + 4 * c, 64))
    at_xy = x * 4 + y
    in_xy = []
    for kx in range(NX):
        for ky in (2, 1, 3, 0):
            if kx + ky:
                ox, oy = lax.rem(x + kx, NX), lax.rem(y + ky, NY)
                in_xy.append((ox * 4 + oy, device(ox, zh, oy, zl, c), ox, oy))
    at_z = zh * 8 + zl
    in_z = []
    for k in (8, 7, 9, 6, 10, 5, 11, 4, 12, 3, 13, 2, 14, 1, 15):
        o = lax.rem(at_z + k, 16)
        in_z.append((o, device(x, lax.div(o, 8), y, lax.rem(o, 8), c)))
    arrived = greet(
        [p for _, p in in_line]
        + [to_far, ahead, behind]
        + [in_xy[k - 1][1] for k in range(4, 16)]
        + [p for _, p in in_plane]
    )

    loads = [
        pltpu.make_async_copy(source, target, local_sem.at[k])
        for k, (source, target) in enumerate(
            (
                (lat_hbm, lat),
                (wt_hbm, wtm.at[pl.ds(12 * dp, 12)]),
                (ws_hbm, wsp.at[pl.ds(36 * dp, 36)]),
                (cot_hbm, cot),
                (gain_hbm, gain),
                (bias_hbm, bias),
            )
        )
    ]
    for copy in loads:
        copy.start()

    pending = []

    def send(ref, target, recv, where):
        copy = remote(ref, target, send_sem.at[len(pending)], recv, where)
        copy.start()
        pending.append(copy)

    drained = [0]

    def drain():
        for copy in pending[drained[0] :]:
            copy.wait_send()
        drained[0] = len(pending)

    def receive(ref, recv):
        remote(ref, ref, send_sem.at[0], recv, to_c).wait_recv()

    def exchange(slots, recv, at, peers):
        for _, target in peers:
            send(slots.at[at], slots.at[at], recv.at[at], target)

    def gathered(slots, recv, peers):
        for other, _ in peers:
            receive(slots.at[other], recv.at[other])

    loads[0].wait()
    wide_lat = lat[...].astype(F32)
    plane[mine, 0:1, :] = jnp.sum(wide_lat, axis=0, keepdims=True)
    plane[mine, 1:2, :] = jnp.sum(wide_lat * wide_lat, axis=0, keepdims=True)
    for copy in loads[1:]:
        copy.wait()
    arrived()

    def t_shard(hi, at):
        return wtm.at[pl.ds(12 * (2 * at + hi), 12)]

    def t_piece(at, quarter):
        return wtm.at[pl.ds(12 * (2 * at + 1 - zh) + 3 * quarter, 3)]

    def s_shard(hi, at, lanes):
        return wsp.at[pl.ds(36 * (2 * at + hi), 36), :, lanes]

    def s_piece(at, quarter, lanes):
        return wsp.at[pl.ds(36 * (2 * at + 1 - zh) + 9 * quarter, 9), :, lanes]

    part = wtm.at[pl.ds(12 * dp + 3 * y, 3)]
    send(part, part, tz_recv.at[0], to_far)
    exchange(plane, plane_recv, mine, in_plane)
    lanes = pl.ds(pl.multiple_of(c * HALF, HALF), HALF)
    part = wsp.at[pl.ds(36 * dp + 9 * y, 9), :, lanes]
    send(part, part, sz_recv.at[0], to_far)
    for target in to_x:
        send(t_shard(zh, x), t_shard(zh, x), tx_recv.at[x], target)
    send(lat, lat, mate_recv.at[0], to_c)
    send(cot, cot, mate_recv.at[1], to_c)
    send(frames.at[edge_out], frames.at[edge_in], halo_recv.at[0], edge_to)
    part = s_shard(zh, x, lanes)
    for target in to_x:
        send(part, part, sx_recv.at[x], target)

    gathered(plane, plane_recv, in_plane)
    line[zl] = total(plane, 8)
    exchange(line, line_recv, zl, in_line)

    part = t_piece(x, y)
    receive(part, tz_recv.at[0])
    for _, target, _, _ in in_xy:
        send(part, part, txy_recv.at[at_xy], target)
    part = s_piece(x, y, lanes)
    receive(part, sz_recv.at[0])
    for _, target, _, _ in in_xy:
        send(part, part, sxy_recv.at[at_xy], target)
    receive(frames.at[edge_in], halo_recv.at[0])
    send(frames.at[edge_in], frames.at[edge_in], pass_recv.at[0], to_c)
    for o in others_x:
        part = s_shard(zh, o, lanes)
        receive(part, sx_recv.at[o])
        send(part, part, c1_recv.at[o], to_c)
    receive(frames.at[2 - c], mate_recv.at[0])
    receive(frames.at[4 - c], mate_recv.at[1])
    order = permutation(c)
    for k in range(2):
        cot_t[:, k * ROWS : (k + 1) * ROWS] = times_transpose(order, frames[3 + k]).astype(BF16)

    gathered(line, line_recv, in_line)
    sums = group_totals(total(line, 8)) / (FRAMES_CELLS * (C // GROUPS))
    mean = sums[0:1]
    inv = 1.0 / jnp.sqrt(sums[1:2] - mean * mean + EPSILON)
    gains, biases = gain[...], bias[...]

    def normed_of(values):
        whitened = (values.astype(F32) - mean) * inv
        return whitened, whitened * gains + biases

    for k in (1, 2):
        _, normed = normed_of(frames[k])
        fill_windows(
            windows.at[k * ROWS : (k + 1) * ROWS, :], normed * jax.nn.sigmoid(normed), 1
        )

    receive(frames.at[5 * c], pass_recv.at[0])
    last = frames[5]
    later = jnp.where(wide < 62, last.astype(F32), 0.0).astype(BF16)
    for o in others_x:
        receive(t_shard(zh, o), tx_recv.at[o])
    for slot, _, ox, oy in in_xy:
        receive(t_piece(ox, oy), txy_recv.at[slot])
    held = jnp.concatenate([frames[3], frames[4], later], axis=0)
    running = jnp.zeros((2 * ROWS, C), F32)
    for delay in range(3):
        start = delay * CELLS
        running = running + times_transpose(
            held[start : start + 2 * ROWS], wtm[delay * 32 : (delay + 1) * 32].reshape(C, C)
        )
    grad_act[...] = running.astype(BF16)
    act_t = times_transpose(order, grad_act[...]).astype(BF16)

    def scatter(left, right, slots, slots_in, recv, tiles):
        for k in (2, 0, 1, 3):
            o = lax.rem(x + k, NX)
            odd_o = lax.rem(o, 2)
            first = lax.div((2 * tiles + 1) * o + 1, 2)
            whole = jnp.dot(
                left,
                right(pl.ds(pl.multiple_of(first * 128, 128), tiles * 128)),
                preferred_element_type=F32,
            ).astype(BF16)
            at_half = first + tiles - (tiles + 1) * odd_o
            half = jnp.dot(
                left, right(pl.ds(pl.multiple_of(at_half * 128, 128), 128)), preferred_element_type=F32
            )
            turned = pltpu.roll(half, 64, 1)
            low = jnp.where(odd_o == 1, turned, half)
            high = jnp.where(odd_o == 1, half, turned)
            left_half = lax.broadcasted_iota(jnp.int32, (16, 128), 1) < 64
            for p in range(NY):
                slot = o * 4 + p
                for tile in range(tiles):
                    slots[slot, tile * 32 : (tile + 1) * 32, :] = whole[
                        p * 32 : (p + 1) * 32, tile * 128 : (tile + 1) * 128
                    ]
                slots[slot, tiles * 32 :, :] = jnp.where(
                    left_half, low[p * 32 : p * 32 + 16], high[p * 32 + 16 : (p + 1) * 32]
                ).astype(BF16)
            for slot, target, _, _ in in_xy[max(4 * k - 1, 0) : 4 * k + 3]:
                send(slots.at[slot], slots_in.at[at_xy], recv.at[at_xy], target)

    def pass_weights(k, o):
        for slot, _, ox, oy in in_xy[max(4 * k - 1, 0) : 4 * k + 3]:
            receive(s_piece(ox, oy, lanes), sxy_recv.at[slot])
        part = s_shard(1 - zh, o, lanes)
        send(part, part, c2_recv.at[o], to_c)

    scatter(act_t, lambda at: windows[ROWS:, at], s1, s1_in, s1_recv, S_TILES)

    own_rows = pl.ds(pl.multiple_of(c * ROWS, ROWS), ROWS)
    fill_windows(adjoint, grad_act[own_rows, :].astype(F32), -1)
    _, normed = normed_of(frames[0])
    fill_windows(windows.at[0:ROWS, :], normed * jax.nn.sigmoid(normed), 1)

    for k in (1, 2, 3, 0):
        pass_weights(k, lax.rem(x + k, NX))
    other_lanes = pl.ds(pl.multiple_of((1 - c) * HALF, HALF), HALF)
    for o in others_x:
        receive(s_shard(zh, o, other_lanes), c1_recv.at[o])
    for o in range(NX):
        receive(s_shard(1 - zh, o, other_lanes), c2_recv.at[o])

    running = jnp.zeros((ROWS, C), F32)
    for tap in range(9):
        taps = slice(tap * C, (tap + 1) * C)
        running = running + times_transpose(
            adjoint[:, taps], wsp[tap * 32 : (tap + 1) * 32].reshape(C, C)
        )
    whitened, normed = normed_of(lat[...])
    sigmoid = jax.nn.sigmoid(normed)
    grad_normed = running * (sigmoid * (1.0 + normed * (1.0 - sigmoid)))
    plane_b[mine, 0:1, :] = jnp.sum(grad_normed * whitened, axis=0, keepdims=True)
    plane_b[mine, 1:2, :] = jnp.sum(grad_normed, axis=0, keepdims=True)
    exchange(plane_b, plane_b_recv, mine, in_plane)
    grad_white = grad_normed * gains

    conv = jnp.dot(windows[...], wsp[...].reshape(9 * C, C), preferred_element_type=F32)
    spatial[ROWS:, :] = conv[ROWS:].astype(BF16)
    spatial[:ROWS, :] = jnp.where(wide > 1, conv[:ROWS], 0.0).astype(BF16)
    for delay in range(3):
        start = (2 - delay) * CELLS
        mixed[:, delay * C : (delay + 1) * C] = spatial[start : start + 2 * ROWS, :]
    scatter(cot_t[...], lambda at: mixed[:, at], t1, t1_in, t1_recv, T_TILES)
    gathered(plane_b, plane_b_recv, in_plane)
    sums_b = total(plane_b, 8)
    line_b[zl] = sums_b
    row_b[x] = sums_b
    exchange(line_b, line_b_recv, zl, in_line)
    for target in to_x:
        send(row_b.at[x], row_b.at[x], row_b_recv.at[x], target)
    temporal = jnp.dot(
        mixed[own_rows, :], wtm[...].reshape(3 * C, C), preferred_element_type=F32
    )
    block_out[...] = (lat[...].astype(F32) + temporal).astype(BF16)


    odd = lax.rem(x, 2)

    def across_z(slots, slots_in, recv, source, source_in, source_recv, tiles, width):
        joined = source[at_xy].astype(F32)
        for slot, _, _, _ in in_xy:
            receive(source_in.at[slot], source_recv.at[slot])
            joined = joined + source_in[slot].astype(F32)
        whole = [joined[tile * 32 : (tile + 1) * 32] for tile in range(tiles)]
        fold = joined[tiles * 32 :]
        half = jnp.concatenate([fold[:, :64], fold[:, 64:]], axis=0)
        columns = jnp.where(
            odd == 1,
            jnp.concatenate([half] + whole, axis=1),
            jnp.concatenate(whole + [half], axis=1),
        )
        for hi in range(NZH):
            mid = columns[:, width * hi : width * (hi + 1)]
            for q in range(8):
                slots[hi * 8 + q, :, 0:width] = mid[q * 4 : (q + 1) * 4].astype(BF16)
                slots[hi * 8 + q, :, width:] = jnp.zeros((4, slots.shape[2] - width), BF16)
        for o, target in in_z:
            send(slots.at[o], slots_in.at[at_z], recv.at[at_z], target)

    scale = 1.0 / math.sqrt(131072)

    def at_last(slots, slots_in, recv, out):
        result = slots[at_z].astype(F32)
        for o, _ in in_z:
            receive(slots_in.at[o], recv.at[o])
            result = result + slots_in[o].astype(F32)
        out[...] = result * scale

    across_z(zs, zs_in, zs_recv, s1, s1_in, s1_recv, S_TILES, 288)
    across_z(zt, zt_in, zt_recv, t1, t1_in, t1_recv, T_TILES, 96)
    for o in others_x:
        receive(row_b.at[o], row_b_recv.at[o])
    both = total(row_b, 4)
    deep_b[at_z] = jnp.where(y < 2, both[:, :HALF], both[:, HALF:])
    for _, target in in_z:
        send(deep_b.at[at_z], deep_b.at[at_z], deep_b_recv.at[at_z], target)

    drain()
    gathered(line_b, line_b_recv, in_line)
    means = group_totals(total(line_b, 8) * gains) / (FRAMES_CELLS * (C // GROUPS))
    inner = (grad_white - means[1:2] - whitened * means[0:1]) * inv
    grad_latents[...] = (cot[...].astype(F32) + inner).astype(BF16)

    at_last(zs, zs_in, zs_recv, s_out)
    for o, _ in in_z:
        receive(deep_b.at[o], deep_b_recv.at[o])
    norm_out[...] = total(deep_b, 16) * scale
    at_last(zt, zt_in, zt_recv, t_out)
    drain()


MAIN_OUTS = (
    ((ROWS, C), BF16), ((ROWS, C), BF16), ((4, 384), F32), ((4, 128), F32), ((2, HALF), F32),
)


def main(lat, cot, ws, wt, gain, bias):
    hbm = pl.BlockSpec(memory_space=pltpu.HBM)
    dma = pltpu.SemaphoreType.DMA
    V = pltpu.VMEM
    return pl.pallas_call(
        main_kernel,
        name="main",
        out_shape=[jax.ShapeDtypeStruct(*shape) for shape in MAIN_OUTS],
        in_specs=[hbm] * 6,
        out_specs=[pl.BlockSpec(memory_space=pltpu.VMEM)] * 5,
        scratch_shapes=[
            V((6, ROWS, C), BF16), V((1, C), F32), V((1, C), F32),
            V((8 * 36, 8, C), BF16), V((8 * 12, 8, C), BF16),
            V((8, 2, C), F32), V((8, 2, C), F32), V((8, 2, C), F32), V((8, 2, C), F32),
            V((NX, 2, C), F32), V((16, 2, HALF), F32),
            V((3 * ROWS, 9 * C), BF16), V((3 * ROWS, C), BF16), V((2 * ROWS, 3 * C), BF16),
            V((2 * ROWS, C), BF16), V((ROWS, 9 * C), BF16), V((HALF, 2 * ROWS), BF16),
            V((16, 32 * S_TILES + 16, 128), BF16), V((16, 32 * S_TILES + 16, 128), BF16),
            V((16, 32 * T_TILES + 16, 128), BF16), V((16, 32 * T_TILES + 16, 128), BF16),
            V((16, 4, 384), BF16), V((16, 4, 384), BF16),
            V((16, 4, 128), BF16), V((16, 4, 128), BF16),
            dma((6,)), dma((SENDS,)),
            dma((8,)), dma((8,)), dma((8,)), dma((8,)), dma((4,)), dma((16,)),
            dma((2,)), dma((1,)), dma((1,)), dma((4,)), dma((1,)), dma((16,)),
            dma((4,)), dma((1,)), dma((16,)), dma((4,)), dma((4,)),
            dma((16,)), dma((16,)), dma((16,)), dma((16,)),
        ],
        compiler_params=pltpu.CompilerParams(
            collective_id=1, has_side_effects=True, vmem_limit_bytes=VMEM_BYTES
        ),
    )(*[pltpu.with_memory_space_constraint(a, pltpu.HBM) for a in (lat, cot, ws, wt, gain, bias)])


def finish_kernel(
    block_out, grad_latents, sums_s, sums_t, norms,
    out_hbm, latents_hbm, spatial_hbm, temporal_hbm, norm_hbm,
    spatial, temporal, norm, store_sem,
):
    wide = lax.axis_index("wide")
    stores = [
        pltpu.make_async_copy(source, target, store_sem.at[k])
        for k, (source, target) in enumerate(
            (
                (block_out, out_hbm),
                (grad_latents, latents_hbm),
                (spatial, spatial_hbm),
                (temporal, temporal_hbm),
                (norm, norm_hbm),
            )
        )
    ]
    stores[0].start()
    stores[1].start()
    spatial[...] = sums_s[:, :288]
    stores[2].start()
    temporal[...] = sums_t[:, :96]
    stores[3].start()
    lane = lax.broadcasted_iota(jnp.int32, (2, HALF), 1)
    for k in range(4):
        norm[:, k : k + 1] = jnp.sum(
            jnp.where(lane == lax.rem(4 * wide, HALF) + k, norms[...], 0.0), axis=1, keepdims=True
        )
    stores[4].start()
    for copy in stores:
        copy.wait()


def finish(*parts):
    hbm = pl.BlockSpec(memory_space=pltpu.HBM)
    dma = pltpu.SemaphoreType.DMA
    last = [((4, 288), F32), ((4, 96), F32), ((2, 4), F32)]
    return pl.pallas_call(
        finish_kernel,
        name="finish",
        out_shape=[jax.ShapeDtypeStruct(*shape) for shape in list(MAIN_OUTS[:2]) + last],
        in_specs=[pl.BlockSpec(memory_space=pltpu.VMEM)] * 5,
        out_specs=[hbm] * 5,
        scratch_shapes=[pltpu.VMEM(*shape) for shape in last] + [dma((5,))],
        compiler_params=pltpu.CompilerParams(vmem_limit_bytes=2 << 20),
    )(*parts)


def local(latents, cotangent, norm_gain, norm_bias, w_spatial, w_temporal):
    block_out, grad_latents, spatial, temporal, norm = finish(
        *main(
            latents.reshape(ROWS, C),
            cotangent.reshape(ROWS, C),
            w_spatial.reshape(36, 8, C),
            w_temporal.reshape(12, 8, C),
            norm_gain.reshape(1, C),
            norm_bias.reshape(1, C),
        )
    )
    return (
        block_out.reshape(latents.shape),
        grad_latents.reshape(latents.shape),
        spatial.T,
        temporal.T,
        norm,
    )


def solution(mesh):
    return jax.shard_map(
        local,
        mesh=mesh,
        in_specs=(
            P("dp", "wide", None, None, None),
            P("dp", "wide", None, None, None),
            P(),
            P(),
            P("dp", None),
            P("dp", None),
        ),
        out_specs=(
            P("dp", "wide", None, None, None),
            P("dp", "wide", None, None, None),
            P("dp", "wide"),
            P("dp", "wide"),
            P(None, "wide"),
        ),
        check_vma=False,
    )
```
